128 devices in a mesh: grp: 4 (over y), mem: 32 (over x, z, core).
Axes of the slice: x: 4, y: 4, z: 4, core: 2. Of those that a mesh axis runs over, the one named last changes fastest.
Arguments:
- pno: bfloat16 [4096, 512, 128], P(('grp', 'mem')), may hold values from -0.5 to 0.5
- amplitudes: bfloat16 [4096, 128, 128], P(('grp', 'mem')), may hold values from -6 to 6
- pno_count: int32 [4096], P(('grp', 'mem')), may hold values from 64 to 128
- pao_coupling: bfloat16 [512, 512], replicated, may hold values from -0.25 to 0.25
- row_owner: int32 [8192, 1], P(('grp', 'mem')), may hold values from 0 to 31; in each aligned block of 64 rows (0 to 63, 64 to 127, ...) at most 4 rows name the same one
- row_pair: int32 [8192], P(('grp', 'mem')), may hold values from 0 to 31
- row_target: int32 [8192], P(('grp', 'mem')), may hold values from 0 to 31
- row_coef: float32 [8192], P(('grp', 'mem')), may hold values from -6 to 6
- column_owner: int32 [2048, 1], P(('grp', 'mem')), may hold values from 0 to 3; in each aligned block of 16 rows (0 to 15, 16 to 31, ...) at most 8 rows name the same one
- column_pair: int32 [2048], P(('grp', 'mem')), may hold values from 0 to 31
- column_target: int32 [2048], P(('grp', 'mem')), may hold values from 0 to 31
- column_coef: float32 [2048], P(('grp', 'mem')), may hold values from -6 to 6
Outputs:
- coupling_residual: float32 [4096, 128, 128], P(('grp', 'mem'))
The draws below stay inside these ranges and needn't reach their ends.
Inputs may be any that keep to these rules, and one draw needn't show every extreme that they name: `row_owner`: among one device's in-group couplings at most 4 name the same member index, and some device's rows reach it. `column_owner`: among one device's cross-group couplings at most 8 name the same group index, and some device's rows reach it.
All inputs are finite; a program needn't handle non-finite values.
Results may differ from the reference program's by a relative error of at most 0.0064.
Values may be sent and summed in bfloat16 or wider, within the bound.
A program may use at most 128 MiB of HBM per device.

```python
import math
import jax
import jax.numpy as jnp
import numpy as np
from jax import lax

K = 512
P_SIZE = 128
PAIR_DEV = 32
TASK_DEV = 64
COL_DEV = 16
CAP_M = 4
CAP_G = 8
PAIRS = 4096
TASKS = 8192
COLS = 2048
N_GRP = 4
N_MEM = 32


def with_ends(drawn, own_key, least, largest):
    longest = drawn.shape.index(max(drawn.shape))
    spots = []
    for shift in (0, 1):
        where = [jax.random.randint(jax.random.fold_in(own_key, axis), (), 0, length) for axis, length in enumerate(drawn.shape)]
        where[longest] = (where[longest] + shift) % drawn.shape[longest]
        spots.append(tuple(where))
    return drawn.at[spots[0]].set(least).at[spots[1]].set(largest)


def block_levels(stream_key, dims, pieces, least, high):
    loudness, own = 1.0, jax.random.fold_in(stream_key, 6)
    for axis_at, parts in pieces:
        draws = jnp.exp(jax.random.uniform(jax.random.fold_in(own, axis_at), (parts,), jnp.float32, least / len(pieces), high / len(pieces)))
        loudness = loudness * jnp.repeat(draws, dims[axis_at] // parts).reshape([-1 if axis == axis_at else 1 for axis in range(len(dims))])
    return loudness


def deal_out(stream_key, own, number, rows, number_of, top, limit, slope):
    sequence = jax.random.permutation(stream_key, number_of)
    crowded, common = shares(number_of, rows * top, limit, slope, True), shares(number_of, rows * top, limit, slope, False)
    places = jnp.arange(number_of)

    def named(lengths, rotation):
        used = int((lengths > 0).sum())
        fixed = max(1, used // 4)
        passed = fixed + (places - fixed + rotation * (used - fixed)) % max(1, number_of - fixed)
        return jnp.zeros((number_of,), jnp.int32).at[sequence[jnp.where(places < fixed, places, passed)]].set(jnp.asarray(lengths, jnp.int32))

    lengths = jnp.where(number % 4 == 0, named(crowded, number // 4), named(common, number - number // 4 - 1))
    mixed = jax.random.permutation(jax.random.fold_in(own, 3), number_of)
    source_of, receiver = mixed[0:number_of // 2 * 2:2], mixed[1:number_of // 2 * 2:2]
    slack = jnp.minimum(lengths[source_of] - 1, limit - lengths[receiver]) // 2
    slack = jnp.where((source_of == sequence[0]) | (receiver == sequence[0]) | (lengths[receiver] == 0), 0, jnp.maximum(slack, 0))
    passed = jax.random.randint(jax.random.fold_in(own, 4), (number_of // 2,), 0, 1 << 20) % (slack + 1)
    lengths = lengths.at[source_of].add(-passed).at[receiver].add(passed)
    items = jnp.searchsorted(jnp.cumsum(lengths), jnp.arange(rows * top), side="right").astype(jnp.int32)
    grid = items.reshape(top, rows).T
    grid = grid[jax.random.permutation(jax.random.fold_in(own, 1), rows)]
    rotation = jax.random.randint(jax.random.fold_in(own, 2), (rows, 1), 0, top)
    return jnp.take_along_axis(grid, (jnp.arange(top)[None, :] + rotation) % top, axis=1)


def shares(number_of, total, most, skew, full):
    weights = [(1 << 20) // math.isqrt(grade ** skew) + 1 for grade in range(1, number_of + 1)]
    largest = most if full else min(most, max(-(-total // number_of), total * weights[0] // sum(weights)))
    least = 1 if total - largest >= number_of - 1 else 0
    counts, rest = [largest] + [least] * (number_of - 1), total - largest - least * (number_of - 1)
    while rest > 0:
        candidates = [i for i in range(1, number_of) if counts[i] < largest] or [i for i in range(1, number_of) if counts[i] < most]
        mass, left = sum([weights[i] for i in candidates]), rest
        for i in candidates:
            addition = min(most - counts[i], max(1, left * weights[i] // mass), rest)
            counts[i] = counts[i] + addition
            rest = rest - addition
    return np.array(counts)


def normal_values(stream_key, extent, deviation, limit, cuts=(), kind=jnp.bfloat16):
    level = block_levels(stream_key, extent, cuts, -0.22, 0.18) if cuts else 1.0
    drawn = jax.random.normal(stream_key, extent, jnp.float32) * deviation * level
    return jnp.minimum(jnp.maximum(drawn, -limit), limit).astype(kind)


def setup_inputs(seed: int = 0) -> dict:
    key_of = jax.random.split(jax.random.key(seed), 13)
    pno = normal_values(key_of[0], (PAIRS, K, P_SIZE), 0.0625, 0.5, ((0, 128),))
    amplitudes = normal_values(key_of[1], (PAIRS, P_SIZE, P_SIZE), 1.0, 6.0, ((0, 128),))
    pno_count = with_ends(jax.random.randint(key_of[2], (PAIRS,), P_SIZE // 2, P_SIZE + 1), jax.random.fold_in(key_of[2], 1), P_SIZE // 2, P_SIZE).astype(jnp.int32)
    pao_coupling = normal_values(key_of[3], (K, K), K ** -0.5, 0.25)
    row_owner_keys = jax.random.split(jax.random.fold_in(key_of[4], 1), TASKS // TASK_DEV)
    row_owner_turns = jax.random.permutation(jax.random.fold_in(key_of[4], 3), TASKS // TASK_DEV)
    row_owner = jax.vmap(lambda own, number: deal_out(jax.random.fold_in(key_of[4], 2), own, number, TASK_DEV, N_MEM, 1, CAP_M, 2))(row_owner_keys, row_owner_turns).reshape((TASKS, 1))
    row_pair = with_ends(jax.random.randint(key_of[5], (TASKS,), 0, PAIR_DEV), jax.random.fold_in(key_of[5], 1), 0, PAIR_DEV - 1).astype(jnp.int32)
    row_target = with_ends(jax.random.randint(key_of[6], (TASKS,), 0, PAIR_DEV), jax.random.fold_in(key_of[6], 1), 0, PAIR_DEV - 1).astype(jnp.int32)
    row_coef = normal_values(key_of[7], (TASKS,), 1.0, 6.0, ((0, 128),), jnp.float32)
    column_owner_keys = jax.random.split(jax.random.fold_in(key_of[8], 1), COLS // COL_DEV)
    column_owner_turns = jax.random.permutation(jax.random.fold_in(key_of[8], 3), COLS // COL_DEV)
    column_owner = jax.vmap(lambda own, number: deal_out(jax.random.fold_in(key_of[8], 2), own, number, COL_DEV, N_GRP, 1, CAP_G, 2))(column_owner_keys, column_owner_turns).reshape((COLS, 1))
    column_pair = with_ends(jax.random.randint(key_of[9], (COLS,), 0, PAIR_DEV), jax.random.fold_in(key_of[9], 1), 0, PAIR_DEV - 1).astype(jnp.int32)
    column_target = with_ends(jax.random.randint(key_of[10], (COLS,), 0, PAIR_DEV), jax.random.fold_in(key_of[10], 1), 0, PAIR_DEV - 1).astype(jnp.int32)
    column_coef = normal_values(key_of[11], (COLS,), 1.0, 6.0, ((0, 128),), jnp.float32)
    return dict(pno=pno, amplitudes=amplitudes, pno_count=pno_count, pao_coupling=pao_coupling, row_owner=row_owner, row_pair=row_pair, row_target=row_target, row_coef=row_coef, column_owner=column_owner, column_pair=column_pair, column_target=column_target, column_coef=column_coef)


def masked_blocks(pno, amplitudes, pno_count):
    width = pno.shape[2]
    live = jnp.arange(width, dtype=jnp.int32)[None, :] < pno_count[:, None]
    live_pno = jnp.where(live[:, None, :], pno, jnp.zeros((), pno.dtype))
    live_amp = jnp.where(live[:, :, None] & live[:, None, :], amplitudes, jnp.zeros((), amplitudes.dtype))
    return live_pno, live_amp


def metric_blocks(live_pno, pao_coupling):
    mixed = jnp.einsum('kj,tkp->tjp', pao_coupling.astype(jnp.float32), live_pno.astype(jnp.float32))
    return (live_pno.astype(jnp.float32) + mixed).astype(jnp.bfloat16)


def coupling_terms(metric_rows, source_pno, source_amp):
    intersection = jnp.einsum('tkp,tkq->tpq', metric_rows.astype(jnp.float32), source_pno.astype(jnp.float32)).astype(jnp.bfloat16)
    half = jnp.einsum('tpq,tqr->tpr', intersection.astype(jnp.float32), source_amp.astype(jnp.float32)).astype(jnp.bfloat16)
    return jnp.einsum('tpr,tsr->tps', half.astype(jnp.float32), intersection.astype(jnp.float32))


def pair_total(target, terms):
    onehot = (jnp.arange(PAIR_DEV, dtype=jnp.int32)[:, None] == target[None, :]).astype(jnp.float32)
    return jnp.einsum('at,tps->aps', onehot, terms, precision=lax.Precision.HIGHEST)


def reference(pno, amplitudes, pno_count, pao_coupling, row_owner, row_pair, row_target, row_coef, column_owner, column_pair, column_target, column_coef):
    live_pno, live_amp = masked_blocks(pno, amplitudes, pno_count)
    devices = N_GRP * N_MEM

    def one_device(index):
        group = index // N_MEM
        member = index % N_MEM
        own_pno = lax.dynamic_slice_in_dim(live_pno, (index * PAIR_DEV).astype(jnp.int32), PAIR_DEV, 0)
        metric = metric_blocks(own_pno, pao_coupling)
        start = (index * TASK_DEV).astype(jnp.int32)
        owner_rows = lax.dynamic_slice_in_dim(row_owner, start, TASK_DEV, 0)[:, 0]
        pair_rows = lax.dynamic_slice_in_dim(row_pair, start, TASK_DEV, 0)
        target_rows = lax.dynamic_slice_in_dim(row_target, start, TASK_DEV, 0)
        coef_rows = lax.dynamic_slice_in_dim(row_coef, start, TASK_DEV, 0)
        source_rows = ((group * N_MEM + owner_rows) * PAIR_DEV + pair_rows).astype(jnp.int32)
        row_terms = coupling_terms(metric[target_rows], live_pno[source_rows], live_amp[source_rows])
        row_terms = coef_rows[:, None, None] * row_terms
        begin = (index * COL_DEV).astype(jnp.int32)
        owner_cols = lax.dynamic_slice_in_dim(column_owner, begin, COL_DEV, 0)[:, 0]
        pair_cols = lax.dynamic_slice_in_dim(column_pair, begin, COL_DEV, 0)
        target_cols = lax.dynamic_slice_in_dim(column_target, begin, COL_DEV, 0)
        coef_cols = lax.dynamic_slice_in_dim(column_coef, begin, COL_DEV, 0)
        source_cols = ((owner_cols * N_MEM + member) * PAIR_DEV + pair_cols).astype(jnp.int32)
        col_terms = coupling_terms(metric[target_cols], live_pno[source_cols], live_amp[source_cols])
        col_terms = coef_cols[:, None, None] * col_terms
        return -(pair_total(target_rows, row_terms) + pair_total(target_cols, col_terms))

    result = lax.map(one_device, jnp.arange(devices, dtype=jnp.int32))
    return result.reshape(devices * PAIR_DEV, pno.shape[2], pno.shape[2])
```

```python
import functools

import jax
import jax.numpy as jnp
from jax import lax
from jax.experimental import pallas as pl
from jax.experimental.pallas import tpu as pltpu
from jax.sharding import PartitionSpec as P

MESH = pl.DeviceIdType.MESH
HALF = 16


def gather_kernel(
    pno, amp, ints, flts, mix,
    row_l, row_a, z_l, y_l, y_a, ints_in, flts_in, met,
    mix_v, send_sem, recv_sem,
):
    me = lax.axis_index("mem")
    g = lax.axis_index("grp")
    core = me % 2
    z = (me // 2) % 4
    x = me // 8

    def at(dx, dz, dc):
        nx = (x + dx) % 4
        nz = (z + dz) % 4
        nc = (core + dc) % 2
        return (g, nx * 8 + nz * 2 + nc)

    def up(dg):
        return ((g + dg) % 4, me)

    row = [at(1, 0, 0), at(3, 0, 0), at(2, 0, 0), at(0, 0, 1), at(1, 0, 1), at(3, 0, 1), at(2, 0, 1)]
    col = [at(0, 1, 0), at(0, 3, 0), at(0, 2, 0)]
    tall = [up(1), up(3), up(2)]
    back = {0: 1, 1: 0, 2: 2, 3: 3, 4: 5, 5: 4, 6: 6}

    barrier = pltpu.get_barrier_semaphore()
    peers = row + col + tall
    for d in peers:
        pl.semaphore_signal(barrier, inc=1, device_id=d, device_id_type=MESH)
    pl.semaphore_wait(barrier, len(peers))

    count = [0]
    live = []

    def send(src, dst, dev):
        i = count[0]
        count[0] += 1
        cp = pltpu.make_async_remote_copy(
            src_ref=src, dst_ref=dst, send_sem=send_sem.at[i], recv_sem=recv_sem.at[i],
            device_id=dev, device_id_type=MESH,
        )
        cp.start()
        live.append(cp)
        return cp

    H1 = pl.ds(0, HALF)
    H2 = pl.ds(HALF, HALF)

    def own(dsts, srcs, devs):
        res = {}
        for way, first, second in ((0, H2, H1), (1, H1, H2)):
            slot = 1 - way
            for name, h in (("first", first), ("second", second)):
                for src, dst in zip(srcs, dsts):
                    res.setdefault((slot, name), []).append(
                        send(src.at[h], dst.at[slot, h], devs[way])
                    )
        return res

    for k, d in enumerate(row):
        send(ints, ints_in.at[back[k]], d)
    for k, d in enumerate(col):
        send(ints, ints_in.at[7 + back[k]], d)
        send(flts, flts_in.at[back[k]], d)
    for k, d in enumerate(tall):
        send(ints, ints_in.at[10 + back[k]], d)

    got_z = own([z_l], [pno], col)
    got_x = own([row_l, row_a], [pno, amp], row)
    got_y = own([y_l, y_a], [pno, amp], tall)
    mate = row[3]
    send(pno, row_l.at[3], mate)
    send(amp, row_a.at[3], mate)

    pltpu.sync_copy(mix, mix_v)

    def metric_of(src, dst):
        def body(l_ref, m_ref):
            for u in range(0, 4, 2):
                two = jnp.concatenate([l_ref[u], l_ref[u + 1]], axis=1)
                mixed = jnp.dot(mix_v[...], two, preferred_element_type=jnp.float32)
                full = (two.astype(jnp.float32) + mixed).astype(jnp.bfloat16)
                m_ref[u] = full[:, :128].T
                m_ref[u + 1] = full[:, 128:].T

        pltpu.emit_pipeline(
            body, grid=(8,),
            in_specs=[pl.BlockSpec((4, 512, 128), lambda i: (i, 0, 0))],
            out_specs=[pl.BlockSpec((4, 128, 512), lambda i: (i, 0, 0))],
        )(src, dst)

    metric_of(pno, met.at[0])

    def relay(got, dsts, devs, to_mate):
        out = []
        for slot, h, way in ((1, H2, 0), (0, H1, 1)):
            for cp in got[(slot, "first")]:
                cp.wait_recv()
            for dst in dsts:
                out.append(send(dst.at[slot, h], dst.at[2, h], devs[way]))
            if to_mate:
                for dst in dsts:
                    send(dst.at[slot, h], dst.at[4 + slot, h], mate)
        return out

    far_z = relay(got_z, [z_l], col, False)
    far_x = relay(got_x, [row_l, row_a], row, True)
    far_y = relay(got_y, [y_l, y_a], tall, False)
    for slot in (0, 1):
        for cp in got_z[(slot, "second")]:
            cp.wait_recv()
        metric_of(z_l.at[slot], met.at[1 + slot])
    for slot, h in ((1, H1), (0, H2)):
        for cp in got_x[(slot, "second")]:
            cp.wait_recv()
        for dst in (row_l, row_a):
            send(dst.at[slot, h], dst.at[4 + slot, h], mate)
    for cp in far_z:
        cp.wait_recv()
    metric_of(z_l.at[2], met.at[3])
    for k, h in ((0, H2), (1, H1)):
        for cp in far_x[2 * k:2 * k + 2]:
            cp.wait_recv()
        for dst in (row_l, row_a):
            send(dst.at[2, h], dst.at[6, h], mate)
    waited = set()
    for got in (got_z, got_x):
        for cps in got.values():
            waited.update(id(cp) for cp in cps)
    for slot in (0, 1):
        waited.update(id(cp) for cp in got_y[(slot, "first")])
    waited.update(id(cp) for cp in far_z + far_x)
    for cp in live:
        cp.wait_send()
        if id(cp) not in waited:
            cp.wait_recv()


N_COPY = 17 + 3 + 4 + 8 + 8 + 2 + 2 + 8 + 4 + 4 + 4 - 1


def gather(pno, amp, ints, flts, mix):
    bf = jnp.bfloat16
    any_spec = pl.BlockSpec(memory_space=pl.ANY)
    outs = [
        jax.ShapeDtypeStruct((7, 32, 512, 128), bf),
        jax.ShapeDtypeStruct((7, 32, 128, 128), bf),
        jax.ShapeDtypeStruct((3, 32, 512, 128), bf),
        jax.ShapeDtypeStruct((3, 32, 512, 128), bf),
        jax.ShapeDtypeStruct((3, 32, 128, 128), bf),
        jax.ShapeDtypeStruct((13, 8, 128), jnp.int32),
        jax.ShapeDtypeStruct((3, 8, 128), jnp.float32),
        jax.ShapeDtypeStruct((4, 32, 128, 512), bf),
    ]
    return pl.pallas_call(
        gather_kernel,
        out_shape=outs,
        in_specs=[any_spec] * 5,
        out_specs=[any_spec] * 8,
        scratch_shapes=[
            pltpu.VMEM((512, 512), bf),
            pltpu.SemaphoreType.DMA((72,)),
            pltpu.SemaphoreType.DMA((72,)),
        ],
        compiler_params=pltpu.CompilerParams(collective_id=0, has_side_effects=True),
    )(pno, amp, ints, flts, mix)


UNROLL = 4
DEPTH = 2


def task_kernel(
    ints, ints_in, flts, flts_in,
    pno, amp, row_l, row_a, y_l, y_a, met,
    own_out, far_out,
    acc, l_buf, a_buf, m_buf, t_list, s_list, p_list, q_list, c_list, sem,
):
    me = lax.axis_index("mem")
    g = lax.axis_index("grp")
    core = me % 2
    z = (me // 2) % 4
    x = me // 8

    def int_of(slot, r, c):
        return ints_in[slot, r, c]

    def put(n, keep, target, slot, pair, live_p, live_q, coef):
        t_list[n] = target
        s_list[n] = slot * 32 + pair
        p_list[n] = live_p
        q_list[n] = live_q
        c_list[n] = -coef
        return n + keep

    n = jnp.int32(0)
    for td in range(4):
        def step(t, n, td=td):
            if td == 0:
                owner, pair, target = ints[0, t], ints[0, 64 + t], ints[1, t]
                coef = flts[0, t]
                live_p = ints[1, 64 + target]
            else:
                k = 6 + td
                owner, pair, target = ints_in[k, 0, t], ints_in[k, 0, 64 + t], ints_in[k, 1, t]
                coef = flts_in[td - 1, 0, t]
                live_p = ints_in[k, 1, 64 + target]
            keep = (((owner // 2) % 4) == z).astype(jnp.int32)
            dx = (owner // 8 - x + 4) % 4
            rel = jnp.where(dx == 1, 0, jnp.where(dx == 3, 1, 2))
            same = (owner % 2) == core
            slot = jnp.where(dx == 0, jnp.where(same, 7, 3), jnp.where(same, rel, 4 + rel))
            far = jnp.minimum(slot, 6)
            live_q = jnp.where(slot == 7, ints[1, 64 + pair], ints_in[far, 1, 64 + pair])
            return put(n, keep, td * 32 + target, slot, pair, live_p, live_q, coef)

        n = lax.fori_loop(0, 64, step, n)

    def col_step(t, n):
        owner, pair, target = ints[2, t], ints[2, 16 + t], ints[2, 32 + t]
        coef = flts[0, 64 + t]
        dg = (owner - g + 4) % 4
        rel = jnp.where(dg == 1, 0, jnp.where(dg == 3, 1, 2))
        slot = jnp.where(dg == 0, 7, 8 + rel)
        live_q = jnp.where(dg == 0, ints[1, 64 + pair], ints_in[10 + rel, 1, 64 + pair])
        return put(n, 1, target, slot, pair, ints[1, 64 + target], live_q, coef)

    n = lax.fori_loop(0, 16, col_step, n)
    for u in range(UNROLL):
        put(n + u, 0, 0, 7, 0, 0, 0, jnp.float32(0))
    steps = (n + UNROLL - 1) // UNROLL

    def copies(i, b):
        for u in range(UNROLL):
            k = i * UNROLL + u
            code = s_list[k]
            slot, pair = code // 32, code % 32
            target = t_list[k]
            yield u, slot, pair, target // 32, target % 32

    def start(i, b):
        for u, slot, pair, td, tp in copies(i, b):
            pltpu.make_async_copy(met.at[td, tp], m_buf.at[b, u], sem.at[b, u, 2]).start()

            @pl.when(slot < 7)
            def _():
                pltpu.make_async_copy(row_l.at[slot, pair], l_buf.at[b, u], sem.at[b, u, 0]).start()
                pltpu.make_async_copy(row_a.at[slot, pair], a_buf.at[b, u], sem.at[b, u, 1]).start()

            @pl.when(slot == 7)
            def _():
                pltpu.make_async_copy(pno.at[pair], l_buf.at[b, u], sem.at[b, u, 0]).start()
                pltpu.make_async_copy(amp.at[pair], a_buf.at[b, u], sem.at[b, u, 1]).start()

            @pl.when(slot > 7)
            def _():
                pltpu.make_async_copy(y_l.at[slot - 8, pair], l_buf.at[b, u], sem.at[b, u, 0]).start()
                pltpu.make_async_copy(y_a.at[slot - 8, pair], a_buf.at[b, u], sem.at[b, u, 1]).start()

    def wait(b):
        for u in range(UNROLL):
            pltpu.make_async_copy(met.at[0, 0], m_buf.at[b, u], sem.at[b, u, 2]).wait()
            pltpu.make_async_copy(pno.at[0], l_buf.at[b, u], sem.at[b, u, 0]).wait()
            pltpu.make_async_copy(amp.at[0], a_buf.at[b, u], sem.at[b, u, 1]).wait()

    start(0, 0)
    acc[...] = jnp.zeros_like(acc)
    rows = lax.broadcasted_iota(jnp.int32, (128, 128), 0)
    lanes = lax.broadcasted_iota(jnp.int32, (128, 128), 1)

    def step(i, carry):
        b = i % 2
        wait(b)

        @pl.when(i + 1 < steps)
        def _():
            start(i + 1, 1 - b)

        terms = []
        for u in range(UNROLL):
            k = i * UNROLL + u
            inter = jnp.dot(m_buf[b, u], l_buf[b, u], preferred_element_type=jnp.float32)
            keep = (rows < p_list[k]) & (lanes < q_list[k])
            terms.append(jnp.where(keep, inter, 0.0).astype(jnp.bfloat16))
        halves = [
            jnp.dot(terms[u], a_buf[b, u], preferred_element_type=jnp.float32).astype(jnp.bfloat16)
            for u in range(UNROLL)
        ]
        for u in range(UNROLL):
            k = i * UNROLL + u
            term = lax.dot_general(
                halves[u], terms[u], (((1,), (1,)), ((), ())), preferred_element_type=jnp.float32
            )
            t = t_list[k]
            acc[t] = acc[t] + c_list[k] * term
        return carry

    lax.fori_loop(0, steps, step, 0)
    own_out[...] = acc[0:32]
    far_out[...] = acc[32:128].astype(jnp.bfloat16)


def tasks(ints, ints_in, flts, flts_in, pno, amp, row_l, row_a, y_l, y_a, met):
    bf = jnp.bfloat16
    any_spec = pl.BlockSpec(memory_space=pl.ANY)
    smem = pl.BlockSpec(memory_space=pltpu.SMEM)
    vmem = pl.BlockSpec(memory_space=pltpu.VMEM)
    size = 256 + 16 + UNROLL
    return pl.pallas_call(
        task_kernel,
        out_shape=[
            jax.ShapeDtypeStruct((32, 128, 128), jnp.float32),
            jax.ShapeDtypeStruct((96, 128, 128), bf),
        ],
        in_specs=[smem] * 4 + [any_spec] * 7,
        out_specs=[vmem, vmem],
        scratch_shapes=[
            pltpu.VMEM((128, 128, 128), jnp.float32),
            pltpu.VMEM((2, UNROLL, 512, 128), bf),
            pltpu.VMEM((2, UNROLL, 128, 128), bf),
            pltpu.VMEM((2, UNROLL, 128, 512), bf),
            pltpu.SMEM((size,), jnp.int32),
            pltpu.SMEM((size,), jnp.int32),
            pltpu.SMEM((size,), jnp.int32),
            pltpu.SMEM((size,), jnp.int32),
            pltpu.SMEM((size,), jnp.float32),
            pltpu.SemaphoreType.DMA((2, UNROLL, 3)),
        ],
        compiler_params=pltpu.CompilerParams(vmem_limit_bytes=40 << 20),
    )(ints, ints_in, flts, flts_in, pno, amp, row_l, row_a, y_l, y_a, met)


def shards(
    pno, amplitudes, pno_count, pao_coupling,
    row_owner, row_pair, row_target, row_coef,
    column_owner, column_pair, column_target, column_coef,
):
    zeros = functools.partial(jnp.zeros, dtype=jnp.int32)
    ints = jnp.concatenate([
        row_owner[:, 0], row_pair, row_target, pno_count, zeros((32,)),
        column_owner[:, 0], column_pair, column_target, zeros((80 + 5 * 128,)),
    ]).reshape(8, 128)
    flts = jnp.concatenate(
        [row_coef, column_coef, jnp.zeros((48 + 7 * 128,), jnp.float32)]
    ).reshape(8, 128)
    row_l, row_a, z_l, y_l, y_a, ints_in, flts_in, met = gather(
        pno, amplitudes, ints, flts, pao_coupling.T
    )
    own, far = tasks(ints, ints_in, flts, flts_in, pno, amplitudes, row_l, row_a, y_l, y_a, met)

    def moved(part, dz):
        perm = []
        for m in range(32):
            x, z, c = m // 8, (m // 2) % 4, m % 2
            perm.append((m, x * 8 + ((z + dz) % 4) * 2 + c))
        return lax.ppermute(part, "mem", perm).astype(jnp.float32)

    return own + moved(far[0:32], 1) + moved(far[32:64], 3) + moved(far[64:96], 2)


def solution(mesh):
    both = P(("grp", "mem"))
    in_specs = (
        P(("grp", "mem"), None, None),
        P(("grp", "mem"), None, None),
        both,
        P(),
        P(("grp", "mem"), None),
        both,
        both,
        both,
        P(("grp", "mem"), None),
        both,
        both,
        both,
    )
    out_specs = P(("grp", "mem"), None, None)
    return jax.shard_map(shards, mesh=mesh, in_specs=in_specs, out_specs=out_specs, check_vma=False)
```

```python
import jax
import jax.numpy as jnp
from jax import lax
from jax.experimental import pallas as pl
from jax.experimental.pallas import tpu as pltpu
from jax.sharding import PartitionSpec as P

MESH = pl.DeviceIdType.MESH
BF = jnp.bfloat16
F32 = jnp.float32
I32 = jnp.int32
HALF = 16
PIECE = 8
MATE = 3
FAR, MATE_FAR = 2, 6
OWN = 7
PLUS = (0, 2, 3, 4)


def table_kernel(
    owner, pair, target, coef, c_owner, c_pair, c_target, c_coef, live, ints, flts, fill, c_fill
):
    def clear(i, carry):
        for r in (0, 1, 2, 4):
            ints[r, i] = 0
        flts[0, i] = 0.0
        flts[1, i] = 0.0
        return carry

    lax.fori_loop(0, 128, clear, 0)

    def clear_fill(i, carry):
        fill[i] = 0
        ints[3, i] = live[i]
        return carry

    lax.fori_loop(0, 32, clear_fill, 0)
    for i in range(4):
        c_fill[i] = 0

    def put(t, carry):
        o = owner[t]
        k = fill[o]
        fill[o] = k + 1
        e = o * 4 + k
        p = target[t]
        ints[0, e] = pair[t]
        ints[1, e] = p
        ints[2, e] = live[p]
        flts[0, e] = coef[t]
        return carry

    lax.fori_loop(0, 64, put, 0)

    def c_put(t, carry):
        o = c_owner[t]
        k = c_fill[o]
        c_fill[o] = k + 1
        e = o * 8 + k
        p = c_target[t]
        ints[4, e] = c_pair[t]
        ints[4, 32 + e] = p
        ints[4, 64 + e] = live[p]
        flts[1, e] = c_coef[t]
        return carry

    lax.fori_loop(0, 16, c_put, 0)


def tables(*lists):
    smem = pl.BlockSpec(memory_space=pltpu.SMEM)
    return pl.pallas_call(
        table_kernel,
        out_shape=[jax.ShapeDtypeStruct((8, 128), I32), jax.ShapeDtypeStruct((8, 128), F32)],
        in_specs=[smem] * 9,
        out_specs=[smem] * 2,
        scratch_shapes=[pltpu.SMEM((32,), I32), pltpu.SMEM((4,), I32)],
    )(*lists)


def main_kernel(
    pno, amp, ints, flts, mix,
    own_out, col_out, terms_in, relay_in, row_l, row_a, z_l, y_l, y_a, ints_in, flts_in,
    mix_v, met, chunk_l0, chunk_l1, chunk_a0, chunk_a1, far_l0, far_l1, far_a0, far_a1,
    terms, col_terms, met_buf, ints_s, flts_s, send_sem, recv_sem, load_sem, met_sem, out_sem,
):
    chunks = ((chunk_l0, chunk_a0), (chunk_l1, chunk_a1))
    far = ((far_l0, far_a0), (far_l1, far_a1))
    me = lax.axis_index("mem")
    g = lax.axis_index("grp")
    core = me % 2
    z = (me // 2) % 4
    x = me // 8

    def member(dx, dz, dc):
        return ((x + dx) % 4) * 8 + ((z + dz) % 4) * 2 + (core + dc) % 2

    def up(dg):
        return ((g + dg) % 4, me)

    row_m = [member(1, 0, 0), member(3, 0, 0), member(2, 0, 0), member(0, 0, 1),
             member(1, 0, 1), member(3, 0, 1), member(2, 0, 1), me]
    row = [(g, m) for m in row_m[:7]]
    col = [(g, member(0, d, 0)) for d in (1, 3, 2)]
    tall = [up(1), up(3), up(2)]
    back = (1, 0, 2, 3, 5, 4, 6)
    mate = row[MATE]

    barrier = pltpu.get_barrier_semaphore()
    peers = row + col + tall
    for d in peers:
        pl.semaphore_signal(barrier, inc=1, device_id=d, device_id_type=MESH)
    pl.semaphore_wait(barrier, len(peers))

    live = []
    arrived = set()

    def send(src, dst, dev):
        i = len(live)
        cp = pltpu.make_async_remote_copy(
            src_ref=src, dst_ref=dst, send_sem=send_sem.at[i], recv_sem=recv_sem.at[i],
            device_id=dev, device_id_type=MESH,
        )
        cp.start()
        live.append(cp)
        return cp

    def arrive(cps):
        for cp in cps:
            cp.wait_recv()
            arrived.add(id(cp))

    local = []

    def keep(src, dst):
        cp = pltpu.make_async_copy(src, dst, out_sem.at[len(local)])
        cp.start()
        local.append(cp)

    H1 = pl.ds(0, HALF)
    H2 = pl.ds(HALF, HALF)

    def own(dsts, srcs, devs):
        res = {}
        for way, order in ((0, (H2, H1)), (1, (H1, H2))):
            for n, h in enumerate(order):
                res[(1 - way, n)] = [
                    send(src.at[h], dst.at[1 - way, h], devs[way]) for src, dst in zip(srcs, dsts)
                ]
        return res

    riders = []
    for k, d in enumerate(row):
        riders.append(send(ints, ints_in.at[back[k]], d))
    for k, d in enumerate(col):
        riders.append(send(ints, ints_in.at[7 + back[k]], d))
        riders.append(send(flts, flts_in.at[back[k]], d))
    for k, d in enumerate(tall):
        riders.append(send(ints, ints_in.at[10 + back[k]], d))
    got_x = own([row_l, row_a], [pno, amp], row)
    got_z = own([z_l], [pno], col)
    got_y = own([y_l, y_a], [pno, amp], tall)
    got_mate = [send(pno, row_l.at[MATE], mate), send(amp, row_a.at[MATE], mate)]

    pltpu.sync_copy(mix, mix_v)

    def metric_of(src, zt):
        def load(i, b):
            return pltpu.make_async_copy(src.at[pl.ds(i * 4, 4)], met_buf.at[b], met_sem.at[b])

        load(0, 0).start()

        def step(i, carry):
            b = i % 2
            load(i, b).wait()

            @pl.when(i < 7)
            def _():
                load(i + 1, 1 - b).start()

            for u in (0, 2):
                two = jnp.concatenate([met_buf[b, u], met_buf[b, u + 1]], axis=1)
                mixed = jnp.dot(mix_v[...], two, preferred_element_type=F32)
                full = (two.astype(F32) + mixed).astype(BF)
                met[zt, i * 4 + u] = full[:, :128].T
                met[zt, i * 4 + u + 1] = full[:, 128:].T
            return carry

        lax.fori_loop(0, 8, step, 0)

    rows = lax.broadcasted_iota(I32, (128, 128), 0)
    lanes = lax.broadcasted_iota(I32, (128, 128), 1)

    def four(spots, lref, aref, store):
        inters, halves = [], []
        for zt, t, p, live_p, live_q, coef in spots:
            inter = jnp.dot(met[zt, t], lref[p], preferred_element_type=F32)
            ok = (rows < live_p) & (lanes < live_q)
            inters.append(jnp.where(ok, inter, 0.0).astype(BF))
        for (zt, t, p, live_p, live_q, coef), inter in zip(spots, inters):
            halves.append(jnp.dot(inter, aref[p], preferred_element_type=F32).astype(BF))
        for n, (spot, inter, half) in enumerate(zip(spots, inters, halves)):
            term = lax.dot_general(half, inter, (((1,), (1,)), ((), ())), preferred_element_type=F32)
            store(n, (-spot[5] * term).astype(BF))

    def row_slots(j, lref, aref, zt):
        spots = []
        for k in range(4):
            e = row_m[j] * 4 + k
            p = ints_s[7 + zt, 0, e]
            spots.append((zt, ints_s[7 + zt, 1, e], p, ints_s[7 + zt, 2, e], ints_s[j, 3, p],
                          flts_s[zt, 0, e]))

        def store(n, v):
            terms[zt, j, n] = v

        four(spots, lref, aref, store)

    def row_work(j, lref, aref, first, last):
        def step(zt, carry):
            row_slots(j, lref, aref, zt)
            return carry

        lax.fori_loop(first, last, step, 0)

    def col_work(rel, lref, aref):
        group = (g + (0, 1, 3, 2)[rel]) % 4
        src = OWN if rel == 0 else 10 + rel

        def step(q, carry):
            spots = []
            for n in range(4):
                e = group * 8 + q * 4 + n
                p = ints_s[7, 4, e]
                spots.append((0, ints_s[7, 4, 32 + e], p, ints_s[7, 4, 64 + e], ints_s[src, 3, p],
                              flts_s[0, 1, e]))

            def store(n, v):
                col_terms[rel, q * 4 + n] = v

            four(spots, lref, aref, store)
            return carry

        lax.fori_loop(0, 2, step, 0)
        keep(col_terms.at[rel], col_out.at[rel])

    passing = {}

    def give(j, zt):
        if zt == 0:
            keep(terms.at[0, j], own_out.at[j])
        elif zt == 3:
            way = 0 if j in PLUS else 1
            passing[j] = send(terms.at[3, j], relay_in.at[j], col[way])
        else:
            send(terms.at[zt, j], terms_in.at[back[zt - 1], j], col[zt - 1])

    def pass_on(j):
        arrive([passing[j]])
        send(relay_in.at[j], terms_in.at[2, j], col[0 if j in PLUS else 1])

    def blocks_of(j):
        if j == OWN:
            return pno, amp
        return row_l.at[j], row_a.at[j]

    def run(stages, late=()):
        def load(i, fn):
            b = i % 2
            for k, (src, dst) in enumerate(zip(stages[i][0], chunks[b])):
                getattr(pltpu.make_async_copy(src, dst, load_sem.at[b, k]), fn)()

        load(0, "start")
        gifts = list(late)
        for i, (blocks, work, after) in enumerate(stages):
            load(i, "wait")
            if i + 1 < len(stages):
                load(i + 1, "start")
            work(*chunks[i % 2])
            for j, zt in gifts:
                give(j, zt)
            gifts = after
        return gifts

    def row_stage(j, first, last):
        return (blocks_of(j), lambda l, a: row_work(j, l, a, first, last),
                [(j, zt) for zt in range(first, last)])

    def col_stage(rel):
        return (y_l.at[rel - 1], y_a.at[rel - 1]), lambda l, a: col_work(rel, l, a), []

    def relay(got, dsts, devs):
        out = []
        for slot, h, way in ((1, H2, 0), (0, H1, 1)):
            arrive(got[(slot, 0)])
            for dst in dsts:
                out.append(send(dst.at[slot, h], dst.at[2, h], devs[way]))
        return out

    metric_of(pno, 0)
    arrive(riders)
    pltpu.sync_copy(ints_in.at[pl.ds(0, 7)], ints_s.at[pl.ds(0, 7)])
    pltpu.sync_copy(ints, ints_s.at[7])
    pltpu.sync_copy(ints_in.at[pl.ds(7, 6)], ints_s.at[pl.ds(8, 6)])
    pltpu.sync_copy(flts, flts_s.at[0])
    pltpu.sync_copy(flts_in, flts_s.at[pl.ds(1, 3)])
    arrive(got_mate)

    def first_work(l, a):
        row_work(OWN, l, a, 0, 1)
        col_work(0, l, a)

    left = run([((pno, amp), first_work, [(OWN, 0)]), row_stage(MATE, 0, 1)])

    far_z = relay(got_z, [z_l], col)
    far_x = []
    for slot, h, way in ((1, H2, 0), (0, H1, 1)):
        arrive(got_x[(slot, 0)])
        for q in (0, 1):
            part = pl.ds((HALF if way == 0 else 0) + q * PIECE, PIECE)
            far_x.append((part, [
                send(row_l.at[slot, part], far_l0.at[part], row[way]),
                send(row_a.at[slot, part], far_a0.at[part], row[way]),
            ]))
    got_mx = []
    for slot, h in ((1, H2), (0, H1)):
        for dst in (row_l, row_a):
            got_mx.append(send(dst.at[slot, h], dst.at[4 + slot, h], mate))
    far_y = relay(got_y, [y_l, y_a], tall)

    for slot in (0, 1):
        arrive(got_z[(slot, 1)])
        metric_of(z_l.at[slot], 1 + slot)
    left = run([row_stage(OWN, 1, 3), row_stage(MATE, 1, 3)], left)
    for slot, h in ((1, H1), (0, H2)):
        arrive(got_x[(slot, 1)])
        for dst in (row_l, row_a):
            got_mx.append(send(dst.at[slot, h], dst.at[4 + slot, h], mate))
    left = run([row_stage(0, 0, 3), row_stage(1, 0, 3)], left)
    arrive(got_mx)
    for slot in (0, 1):
        arrive(got_y[(slot, 1)])
    left = run([row_stage(4, 0, 3), row_stage(5, 0, 3), col_stage(1), col_stage(2)], left)
    arrive(far_z)
    metric_of(z_l.at[2], 3)
    near = (OWN, MATE, 0, 1, 4, 5)
    left = run([row_stage(j, 3, 4) for j in near], left)
    for j in near[:-1]:
        pass_on(j)
    for j, zt in left:
        give(j, zt)
    pass_on(near[-1])

    mate_far = []
    for part, cps in (far_x[0], far_x[2], far_x[1], far_x[3]):
        arrive(cps)
        for src, dst in zip(*far):
            mate_far.append(send(src.at[part], dst.at[part], mate))
    for n, j in ((0, FAR), (1, MATE_FAR)):
        if n == 1:
            arrive(mate_far)
        row_slots(j, *far[n], 3)
        row_slots(j, *far[n], 1)
        give(j, 3)
        row_slots(j, *far[n], 2)
        give(j, 1)
        row_slots(j, *far[n], 0)
        give(j, 2)
    pass_on(FAR)
    give(FAR, 0)
    give(MATE_FAR, 0)
    pass_on(MATE_FAR)
    arrive(far_y)
    run([col_stage(3)])
    for cp in local:
        cp.wait()
    for cp in live:
        cp.wait_send()
        if id(cp) not in arrived:
            cp.wait_recv()


def main(pno, amp, ints, flts, mix):
    any_spec = pl.BlockSpec(memory_space=pl.ANY)
    shape = jax.ShapeDtypeStruct
    outs = [
        shape((8, 4, 128, 128), BF),
        shape((4, 8, 128, 128), BF),
        shape((3, 8, 4, 128, 128), BF),
        shape((8, 4, 128, 128), BF),
        shape((7, 32, 512, 128), BF),
        shape((7, 32, 128, 128), BF),
        shape((3, 32, 512, 128), BF),
        shape((3, 32, 512, 128), BF),
        shape((3, 32, 128, 128), BF),
        shape((13, 8, 128), I32),
        shape((3, 8, 128), F32),
    ]
    return pl.pallas_call(
        main_kernel,
        out_shape=outs,
        in_specs=[any_spec] * 5,
        out_specs=[any_spec] * len(outs),
        scratch_shapes=[
            pltpu.VMEM((512, 512), BF),
            pltpu.VMEM((4, 32, 128, 512), BF),
            pltpu.VMEM((32, 512, 128), BF),
            pltpu.VMEM((32, 512, 128), BF),
            pltpu.VMEM((32, 128, 128), BF),
            pltpu.VMEM((32, 128, 128), BF),
            pltpu.VMEM((32, 512, 128), BF),
            pltpu.VMEM((32, 512, 128), BF),
            pltpu.VMEM((32, 128, 128), BF),
            pltpu.VMEM((32, 128, 128), BF),
            pltpu.VMEM((4, 8, 4, 128, 128), BF),
            pltpu.VMEM((4, 8, 128, 128), BF),
            pltpu.VMEM((2, 4, 512, 128), BF),
            pltpu.SMEM((14, 8, 128), I32),
            pltpu.SMEM((4, 8, 128), F32),
            pltpu.SemaphoreType.DMA((128,)),
            pltpu.SemaphoreType.DMA((128,)),
            pltpu.SemaphoreType.DMA((2, 2)),
            pltpu.SemaphoreType.DMA((2,)),
            pltpu.SemaphoreType.DMA((16,)),
        ],
        compiler_params=pltpu.CompilerParams(
            collective_id=0, has_side_effects=True, vmem_limit_bytes=63 << 20
        ),
    )(pno, amp, ints, flts, mix)


def sum_kernel(ints, own_terms, col_terms, terms_in, out):
    me = lax.axis_index("mem")
    core = me % 2
    z = (me // 2) % 4
    x = me // 8
    out[...] = jnp.zeros_like(out)
    from_z = (0, 1, 3, 2)
    from_x = (1, 3, 2, 0, 1, 3, 2, 0)
    for j in range(8):
        for zi in range(4):
            m = ((x + from_x[j]) % 4) * 8 + ((z + from_z[zi]) % 4) * 2 + (core + (3 <= j < 7)) % 2
            for k in range(4):
                e = m * 4 + k

                @pl.when(ints[2, e] > 0)
                def _():
                    t = ints[1, e]
                    v = own_terms[j, k] if zi == 0 else terms_in[zi - 1, j, k]
                    out[t] = out[t] + v.astype(F32)

    g = lax.axis_index("grp")
    for rel in range(4):
        for k in range(8):
            e = ((g + (0, 1, 3, 2)[rel]) % 4) * 8 + k

            @pl.when(ints[4, 64 + e] > 0)
            def _():
                t = ints[4, 32 + e]
                out[t] = out[t] + col_terms[rel, k].astype(F32)


def total(ints, own_terms, col_terms, terms_in):
    vmem = pl.BlockSpec(memory_space=pltpu.VMEM)
    return pl.pallas_call(
        sum_kernel,
        out_shape=jax.ShapeDtypeStruct((32, 128, 128), F32),
        in_specs=[pl.BlockSpec(memory_space=pltpu.SMEM)] + [vmem] * 3,
        out_specs=vmem,
    )(ints, own_terms, col_terms, terms_in)


def shards(
    pno, amplitudes, pno_count, pao_coupling,
    row_owner, row_pair, row_target, row_coef,
    column_owner, column_pair, column_target, column_coef,
):
    ints, flts = tables(
        row_owner[:, 0], row_pair, row_target, row_coef,
        column_owner[:, 0], column_pair, column_target, column_coef, pno_count,
    )
    outs = main(pno, amplitudes, ints, flts, pao_coupling.T)
    return total(ints, *outs[:3])


def solution(mesh):
    both = P(("grp", "mem"))
    in_specs = (
        P(("grp", "mem"), None, None),
        P(("grp", "mem"), None, None),
        both,
        P(),
        P(("grp", "mem"), None),
        both,
        both,
        both,
        P(("grp", "mem"), None),
        both,
        both,
        both,
    )
    out_specs = P(("grp", "mem"), None, None)
    return jax.shard_map(shards, mesh=mesh, in_specs=in_specs, out_specs=out_specs, check_vma=False)
```

```python
import jax
import jax.numpy as jnp
from jax import lax
from jax.experimental import pallas as pl
from jax.experimental.pallas import tpu as pltpu
from jax.sharding import PartitionSpec as P

MESH = pl.DeviceIdType.MESH
BF = jnp.bfloat16
F32 = jnp.float32
I32 = jnp.int32
HALF = 16
PIECE = 8
MATE = 3
FAR, MATE_FAR = 2, 6
OWN = 7
PLUS = (0, 2, 3, 4)


def main_kernel(
    pno, amp, mix, *refs,
):
    lists = refs[:9]
    (
        own_out, col_out, terms_in, ints, flts,
        relay_in, row_l, row_a, z_l, y_l, y_a, ints_in, flts_in,
    ) = refs[9:22]
    list_v = refs[22:31]
    (
        wide, tab_i, tab_f, mix_in, mix_v, met,
        chunk_l0, chunk_l1, chunk_a0, chunk_a1, far_l0, far_l1, far_a0, far_a1,
        terms, col_terms, met_buf, ints_s, flts_s, send_sem, recv_sem, load_sem, met_sem,
        out_sem, list_sem,
    ) = refs[31:]
    chunks = ((chunk_l0, chunk_a0), (chunk_l1, chunk_a1))
    far = ((far_l0, far_a0), (far_l1, far_a1))
    me = lax.axis_index("mem")
    g = lax.axis_index("grp")
    core = me % 2
    z = (me // 2) % 4
    x = me // 8

    def member(dx, dz, dc):
        return ((x + dx) % 4) * 8 + ((z + dz) % 4) * 2 + (core + dc) % 2

    def up(dg):
        return ((g + dg) % 4, me)

    row_m = [member(1, 0, 0), member(3, 0, 0), member(2, 0, 0), member(0, 0, 1),
             member(1, 0, 1), member(3, 0, 1), member(2, 0, 1), me]
    row = [(g, m) for m in row_m[:7]]
    col = [(g, member(0, d, 0)) for d in (1, 3, 2)]
    tall = [up(1), up(3), up(2)]
    back = (1, 0, 2, 3, 5, 4, 6)
    mate = row[MATE]

    barrier = pltpu.get_barrier_semaphore()
    peers = row + col + tall
    for d in peers:
        pl.semaphore_signal(barrier, inc=1, device_id=d, device_id_type=MESH)
    pl.semaphore_wait(barrier, len(peers))

    live = []
    arrived = set()

    def send(src, dst, dev):
        i = len(live)
        cp = pltpu.make_async_remote_copy(
            src_ref=src, dst_ref=dst, send_sem=send_sem.at[i], recv_sem=recv_sem.at[i],
            device_id=dev, device_id_type=MESH,
        )
        cp.start()
        live.append(cp)
        return cp

    def arrive(cps):
        for cp in cps:
            cp.wait_recv()
            arrived.add(id(cp))

    local = []

    def keep(src, dst):
        cp = pltpu.make_async_copy(src, dst, out_sem.at[len(local)])
        cp.start()
        local.append(cp)

    H1 = pl.ds(0, HALF)
    H2 = pl.ds(HALF, HALF)

    def own(dsts, srcs, devs):
        res = {}
        for way, order in ((0, (H2, H1)), (1, (H1, H2))):
            for n, h in enumerate(order):
                res[(1 - way, n)] = [
                    send(src.at[h], dst.at[1 - way, h], devs[way]) for src, dst in zip(srcs, dsts)
                ]
        return res

    got_x = own([row_l, row_a], [pno, amp], row)
    got_z = own([z_l], [pno], col)
    got_y = own([y_l, y_a], [pno, amp], tall)
    got_mate = [send(pno, row_l.at[MATE], mate), send(amp, row_a.at[MATE], mate)]

    small = [
        pltpu.make_async_copy(src, dst, list_sem.at[i])
        for i, (src, dst) in enumerate(zip(lists + (mix,), list_v + (mix_in,)))
    ]
    for cp in small:
        cp.start()
    rows = lax.broadcasted_iota(I32, (128, 128), 0)
    lanes = lax.broadcasted_iota(I32, (128, 128), 1)
    wide[...] = jnp.zeros_like(wide)
    for i, cp in enumerate(small[:9]):
        cp.wait()
        wide[i:i + 1, 0:list_v[i].shape[1]] = list_v[i][...].astype(F32)

    def across(i):
        return jnp.broadcast_to(wide[i:i + 1, :], (128, 128))

    def down(i):
        return across(i).T

    def place(owner, first, number, room):
        mine = down(owner)
        same = (mine == across(owner)) & (lanes < rows) & (lanes < number)
        earlier = jnp.sum(jnp.where(same, 1.0, 0.0), axis=1, keepdims=True)
        slot = (mine * room + earlier).astype(I32)
        target = down(first + 2)
        kept = (target.astype(I32) == lanes) & (lanes < 32)
        alive = jnp.sum(jnp.where(kept, across(4), 0.0), axis=1, keepdims=True)
        return slot, (down(first + 1), target, jnp.broadcast_to(alive, (128, 128))), down(first + 3)

    def spread(slot, number, shift, value):
        hit = (slot + shift == lanes) & (rows < number)
        return jnp.sum(jnp.where(hit, value, 0.0), axis=0, keepdims=True)

    slot, parts, coef = place(0, 0, 64, 4)
    tab_i[...] = jnp.zeros_like(tab_i)
    tab_f[...] = jnp.zeros_like(tab_f)
    for r, value in enumerate(parts):
        tab_i[r:r + 1, :] = spread(slot, 64, 0, value).astype(I32)
    tab_f[0:1, :] = spread(slot, 64, 0, coef)
    tab_i[3:4, :] = wide[4:5, :].astype(I32)
    slot, parts, coef = place(5, 5, 16, 8)
    tab_i[4:5, :] = sum(
        spread(slot, 16, 32 * r, value) for r, value in enumerate(parts)
    ).astype(I32)
    tab_f[1:2, :] = spread(slot, 16, 0, coef)
    small[9].wait()
    mix_v[...] = mix_in[...].T
    pltpu.sync_copy(tab_i, ints)
    pltpu.sync_copy(tab_f, flts)

    riders = []
    for k, d in enumerate(row):
        riders.append(send(ints, ints_in.at[back[k]], d))
    for k, d in enumerate(col):
        riders.append(send(ints, ints_in.at[7 + back[k]], d))
        riders.append(send(flts, flts_in.at[back[k]], d))
    for k, d in enumerate(tall):
        riders.append(send(ints, ints_in.at[10 + back[k]], d))

    def metric_of(src, zt):
        def load(i, b):
            return pltpu.make_async_copy(src.at[pl.ds(i * 4, 4)], met_buf.at[b], met_sem.at[b])

        load(0, 0).start()

        def step(i, carry):
            b = i % 2
            load(i, b).wait()

            @pl.when(i < 7)
            def _():
                load(i + 1, 1 - b).start()

            for u in (0, 2):
                two = jnp.concatenate([met_buf[b, u], met_buf[b, u + 1]], axis=1)
                mixed = jnp.dot(mix_v[...], two, preferred_element_type=F32)
                full = (two.astype(F32) + mixed).astype(BF)
                met[zt, i * 4 + u] = full[:, :128].T
                met[zt, i * 4 + u + 1] = full[:, 128:].T
            return carry

        lax.fori_loop(0, 8, step, 0)

    def four(spots, lref, aref, store):
        inters, halves = [], []
        for zt, t, p, live_p, live_q, coef in spots:
            inter = jnp.dot(met[zt, t], lref[p], preferred_element_type=F32)
            ok = (rows < live_p) & (lanes < live_q)
            inters.append(jnp.where(ok, inter, 0.0).astype(BF))
        for (zt, t, p, live_p, live_q, coef), inter in zip(spots, inters):
            halves.append(jnp.dot(inter, aref[p], preferred_element_type=F32).astype(BF))
        for n, (spot, inter, half) in enumerate(zip(spots, inters, halves)):
            term = lax.dot_general(half, inter, (((1,), (1,)), ((), ())), preferred_element_type=F32)
            store(n, (-spot[5] * term).astype(BF))

    def row_slots(j, lref, aref, zt):
        spots = []
        for k in range(4):
            e = row_m[j] * 4 + k
            p = ints_s[7 + zt, 0, e] & 31
            spots.append((zt, ints_s[7 + zt, 1, e] & 31, p, ints_s[7 + zt, 2, e], ints_s[j, 3, p],
                          flts_s[zt, 0, e]))

        def store(n, v):
            terms[zt, j, n] = v

        four(spots, lref, aref, store)

    def row_work(j, lref, aref, first, last):
        def step(zt, carry):
            row_slots(j, lref, aref, zt)
            return carry

        lax.fori_loop(first, last, step, 0)

    def col_work(rel, lref, aref):
        group = (g + (0, 1, 3, 2)[rel]) % 4
        src = OWN if rel == 0 else 10 + rel

        def step(q, carry):
            spots = []
            for n in range(4):
                e = group * 8 + q * 4 + n
                p = ints_s[7, 4, e] & 31
                spots.append((0, ints_s[7, 4, 32 + e] & 31, p, ints_s[7, 4, 64 + e], ints_s[src, 3, p],
                              flts_s[0, 1, e]))

            def store(n, v):
                col_terms[rel, q * 4 + n] = v

            four(spots, lref, aref, store)
            return carry

        lax.fori_loop(0, 2, step, 0)
        keep(col_terms.at[rel], col_out.at[rel])

    passing = {}

    def give(j, zt):
        if zt == 0:
            keep(terms.at[0, j], own_out.at[j])
        elif zt == 3:
            way = 0 if j in PLUS else 1
            passing[j] = send(terms.at[3, j], relay_in.at[j], col[way])
        else:
            send(terms.at[zt, j], terms_in.at[back[zt - 1], j], col[zt - 1])

    def pass_on(j):
        arrive([passing[j]])
        send(relay_in.at[j], terms_in.at[2, j], col[0 if j in PLUS else 1])

    def blocks_of(j):
        if j == OWN:
            return pno, amp
        return row_l.at[j], row_a.at[j]

    def run(stages, late=()):
        def load(i, fn):
            b = i % 2
            for k, (src, dst) in enumerate(zip(stages[i][0], chunks[b])):
                getattr(pltpu.make_async_copy(src, dst, load_sem.at[b, k]), fn)()

        load(0, "start")
        gifts = list(late)
        for i, (blocks, work, after) in enumerate(stages):
            load(i, "wait")
            if i + 1 < len(stages):
                load(i + 1, "start")
            work(*chunks[i % 2])
            for j, zt in gifts:
                give(j, zt)
            gifts = after
        return gifts

    def row_stage(j, first, last):
        return (blocks_of(j), lambda l, a: row_work(j, l, a, first, last),
                [(j, zt) for zt in range(first, last)])

    def col_stage(rel):
        return (y_l.at[rel - 1], y_a.at[rel - 1]), lambda l, a: col_work(rel, l, a), []

    def relay(got, dsts, devs):
        out = []
        for slot, h, way in ((1, H2, 0), (0, H1, 1)):
            arrive(got[(slot, 0)])
            for dst in dsts:
                out.append(send(dst.at[slot, h], dst.at[2, h], devs[way]))
        return out

    metric_of(pno, 0)
    arrive(riders)
    pltpu.sync_copy(ints_in.at[pl.ds(0, 7)], ints_s.at[pl.ds(0, 7)])
    pltpu.sync_copy(ints, ints_s.at[7])
    pltpu.sync_copy(ints_in.at[pl.ds(7, 6)], ints_s.at[pl.ds(8, 6)])
    pltpu.sync_copy(flts, flts_s.at[0])
    pltpu.sync_copy(flts_in, flts_s.at[pl.ds(1, 3)])
    arrive(got_mate)

    def first_work(l, a):
        row_work(OWN, l, a, 0, 1)
        col_work(0, l, a)

    left = run([((pno, amp), first_work, [(OWN, 0)]), row_stage(MATE, 0, 1)])

    far_z = relay(got_z, [z_l], col)
    far_x = []
    for slot, h, way in ((1, H2, 0), (0, H1, 1)):
        arrive(got_x[(slot, 0)])
        for q in (0, 1):
            part = pl.ds((HALF if way == 0 else 0) + q * PIECE, PIECE)
            far_x.append((part, [
                send(row_l.at[slot, part], far_l0.at[part], row[way]),
                send(row_a.at[slot, part], far_a0.at[part], row[way]),
            ]))
    got_mx = []
    for slot, h in ((1, H2), (0, H1)):
        for dst in (row_l, row_a):
            got_mx.append(send(dst.at[slot, h], dst.at[4 + slot, h], mate))
    far_y = relay(got_y, [y_l, y_a], tall)

    for slot in (0, 1):
        arrive(got_z[(slot, 1)])
        metric_of(z_l.at[slot], 1 + slot)
    left = run([row_stage(OWN, 1, 3), row_stage(MATE, 1, 3)], left)
    for slot, h in ((1, H1), (0, H2)):
        arrive(got_x[(slot, 1)])
        for dst in (row_l, row_a):
            got_mx.append(send(dst.at[slot, h], dst.at[4 + slot, h], mate))
    left = run([row_stage(0, 0, 3), row_stage(1, 0, 3)], left)
    arrive(got_mx)
    for slot in (0, 1):
        arrive(got_y[(slot, 1)])
    left = run([row_stage(4, 0, 3), row_stage(5, 0, 3), col_stage(1), col_stage(2)], left)
    arrive(far_z)
    metric_of(z_l.at[2], 3)
    near = (OWN, MATE, 0, 1, 4, 5)
    left = run([row_stage(j, 3, 4) for j in near], left)
    for j in near[:-1]:
        pass_on(j)
    for j, zt in left:
        give(j, zt)
    pass_on(near[-1])

    mate_far = []
    for part, cps in (far_x[0], far_x[2], far_x[1], far_x[3]):
        arrive(cps)
        for src, dst in zip(*far):
            mate_far.append(send(src.at[part], dst.at[part], mate))
    for n, j in ((0, FAR), (1, MATE_FAR)):
        if n == 1:
            arrive(mate_far)
        row_slots(j, *far[n], 3)
        row_slots(j, *far[n], 1)
        give(j, 3)
        row_slots(j, *far[n], 2)
        give(j, 1)
        row_slots(j, *far[n], 0)
        give(j, 2)
    pass_on(FAR)
    give(FAR, 0)
    give(MATE_FAR, 0)
    pass_on(MATE_FAR)
    arrive(far_y)
    run([col_stage(3)])
    for cp in local:
        cp.wait()
    for cp in live:
        cp.wait_send()
        if id(cp) not in arrived:
            cp.wait_recv()


def main(pno, amp, mix, lists):
    any_spec = pl.BlockSpec(memory_space=pl.ANY)
    shape = jax.ShapeDtypeStruct
    outs = [
        shape((8, 4, 128, 128), BF),
        shape((4, 8, 128, 128), BF),
        shape((3, 8, 4, 128, 128), BF),
        shape((8, 128), I32),
        shape((8, 128), F32),
        shape((8, 4, 128, 128), BF),
        shape((7, 32, 512, 128), BF),
        shape((7, 32, 128, 128), BF),
        shape((3, 32, 512, 128), BF),
        shape((3, 32, 512, 128), BF),
        shape((3, 32, 128, 128), BF),
        shape((13, 8, 128), I32),
        shape((3, 8, 128), F32),
    ]
    return pl.pallas_call(
        main_kernel,
        out_shape=outs,
        in_specs=[any_spec] * 12,
        out_specs=[any_spec] * len(outs),
        scratch_shapes=[pltpu.VMEM(v.shape, v.dtype) for v in lists] + [
            pltpu.VMEM((16, 128), F32),
            pltpu.VMEM((8, 128), I32),
            pltpu.VMEM((8, 128), F32),
            pltpu.VMEM((512, 512), BF),
            pltpu.VMEM((512, 512), BF),
            pltpu.VMEM((4, 32, 128, 512), BF),
            pltpu.VMEM((32, 512, 128), BF),
            pltpu.VMEM((32, 512, 128), BF),
            pltpu.VMEM((32, 128, 128), BF),
            pltpu.VMEM((32, 128, 128), BF),
            pltpu.VMEM((32, 512, 128), BF),
            pltpu.VMEM((32, 512, 128), BF),
            pltpu.VMEM((32, 128, 128), BF),
            pltpu.VMEM((32, 128, 128), BF),
            pltpu.VMEM((4, 8, 4, 128, 128), BF),
            pltpu.VMEM((4, 8, 128, 128), BF),
            pltpu.VMEM((2, 4, 512, 128), BF),
            pltpu.SMEM((14, 8, 128), I32),
            pltpu.SMEM((4, 8, 128), F32),
            pltpu.SemaphoreType.DMA((128,)),
            pltpu.SemaphoreType.DMA((128,)),
            pltpu.SemaphoreType.DMA((2, 2)),
            pltpu.SemaphoreType.DMA((2,)),
            pltpu.SemaphoreType.DMA((16,)),
            pltpu.SemaphoreType.DMA((10,)),
        ],
        compiler_params=pltpu.CompilerParams(
            collective_id=0, has_side_effects=True, vmem_limit_bytes=63 << 20
        ),
    )(pno, amp, mix, *lists)


def sum_kernel(ints, own_terms, col_terms, terms_in, out, own_v, col_v, in_v, sem):
    me = lax.axis_index("mem")
    g = lax.axis_index("grp")
    core = me % 2
    z = (me // 2) % 4
    x = me // 8
    loads = [
        pltpu.make_async_copy(own_terms, own_v, sem.at[0]),
        pltpu.make_async_copy(col_terms, col_v, sem.at[1]),
    ] + [pltpu.make_async_copy(terms_in.at[i], in_v.at[i], sem.at[2 + i]) for i in range(3)]
    for cp in loads:
        cp.start()
    out[...] = jnp.zeros_like(out)
    from_z = (0, 1, 3, 2)
    from_x = (1, 3, 2, 0, 1, 3, 2, 0)
    for zi in range(4):
        loads[zi + 1 if zi else 0].wait()
        for j in range(8):
            m = ((x + from_x[j]) % 4) * 8 + ((z + from_z[zi]) % 4) * 2 + (core + (3 <= j < 7)) % 2
            for k in range(4):
                e = m * 4 + k

                @pl.when(ints[2, e] > 0)
                def _():
                    t = ints[1, e]
                    v = own_v[j, k] if zi == 0 else in_v[zi - 1, j, k]
                    out[t] = out[t] + v.astype(F32)

        if zi == 0:
            loads[1].wait()
            for rel in range(4):
                for k in range(8):
                    e = ((g + (0, 1, 3, 2)[rel]) % 4) * 8 + k

                    @pl.when(ints[4, 64 + e] > 0)
                    def _():
                        t = ints[4, 32 + e]
                        out[t] = out[t] + col_v[rel, k].astype(F32)


def total(ints, own_terms, col_terms, terms_in):
    any_spec = pl.BlockSpec(memory_space=pl.ANY)
    return pl.pallas_call(
        sum_kernel,
        out_shape=jax.ShapeDtypeStruct((32, 128, 128), F32),
        in_specs=[pl.BlockSpec(memory_space=pltpu.SMEM)] + [any_spec] * 3,
        out_specs=pl.BlockSpec(memory_space=pltpu.VMEM),
        scratch_shapes=[
            pltpu.VMEM(own_terms.shape, BF),
            pltpu.VMEM(col_terms.shape, BF),
            pltpu.VMEM(terms_in.shape, BF),
            pltpu.SemaphoreType.DMA((5,)),
        ],
        compiler_params=pltpu.CompilerParams(vmem_limit_bytes=63 << 20),
    )(ints, own_terms, col_terms, terms_in)


def shards(
    pno, amplitudes, pno_count, pao_coupling,
    row_owner, row_pair, row_target, row_coef,
    column_owner, column_pair, column_target, column_coef,
):
    lists = [
        v.reshape(1, -1)
        for v in (
            row_owner, row_pair, row_target, row_coef, pno_count,
            column_owner, column_pair, column_target, column_coef,
        )
    ]
    own_terms, col_terms, terms_in, ints = main(pno, amplitudes, pao_coupling, lists)[:4]
    return total(ints, own_terms, col_terms, terms_in)


def solution(mesh):
    both = P(("grp", "mem"))
    in_specs = (
        P(("grp", "mem"), None, None),
        P(("grp", "mem"), None, None),
        both,
        P(),
        P(("grp", "mem"), None),
        both,
        both,
        both,
        P(("grp", "mem"), None),
        both,
        both,
        both,
    )
    out_specs = P(("grp", "mem"), None, None)
    return jax.shard_map(shards, mesh=mesh, in_specs=in_specs, out_specs=out_specs, check_vma=False)
```

```python
import jax
import jax.numpy as jnp
from jax import lax
from jax.experimental import pallas as pl
from jax.experimental.pallas import tpu as pltpu
from jax.sharding import PartitionSpec as P

MESH = pl.DeviceIdType.MESH
BF = jnp.bfloat16
F32 = jnp.float32
I32 = jnp.int32
HALF = 16
PIECE = 8
MATE = 3
FAR, MATE_FAR = 2, 6
OWN = 7
PLUS = (0, 2, 3, 4)


def main_kernel(
    pno, amp, mix, *refs,
):
    lists = refs[:9]
    (
        own_out, col_out, terms_in, ints, flts,
        relay_in, row_l, row_a, z_l, y_l, y_a, ints_in, flts_in,
    ) = refs[9:22]
    list_v = refs[22:31]
    (
        wide, tab_i, tab_f, mix_in, mix_v, met,
        chunk_l0, chunk_l1, chunk_a0, chunk_a1, far_l0, far_l1, far_a0, far_a1,
        terms, col_terms, met_buf, ints_s, flts_s, send_sem, recv_sem, load_sem, met_sem,
        out_sem, list_sem,
    ) = refs[31:]
    chunks = ((chunk_l0, chunk_a0), (chunk_l1, chunk_a1))
    far = ((far_l0, far_a0), (far_l1, far_a1))
    me = lax.axis_index("mem")
    g = lax.axis_index("grp")
    core = me % 2
    z = (me // 2) % 4
    x = me // 8

    def member(dx, dz, dc):
        return ((x + dx) % 4) * 8 + ((z + dz) % 4) * 2 + (core + dc) % 2

    def up(dg):
        return ((g + dg) % 4, me)

    row_m = [member(1, 0, 0), member(3, 0, 0), member(2, 0, 0), member(0, 0, 1),
             member(1, 0, 1), member(3, 0, 1), member(2, 0, 1), me]
    row = [(g, m) for m in row_m[:7]]
    col = [(g, member(0, d, 0)) for d in (1, 3, 2)]
    tall = [up(1), up(3), up(2)]
    back = (1, 0, 2, 3, 5, 4, 6)
    mate = row[MATE]

    live = []
    arrived = set()

    def send(src, dst, dev):
        i = len(live)
        cp = pltpu.make_async_remote_copy(
            src_ref=src, dst_ref=dst, send_sem=send_sem.at[i], recv_sem=recv_sem.at[i],
            device_id=dev, device_id_type=MESH,
        )
        cp.start()
        live.append(cp)
        return cp

    def arrive(cps):
        for cp in cps:
            cp.wait_recv()
            arrived.add(id(cp))

    local = []

    def keep(src, dst):
        cp = pltpu.make_async_copy(src, dst, out_sem.at[len(local)])
        cp.start()
        local.append(cp)

    H1 = pl.ds(0, HALF)
    H2 = pl.ds(HALF, HALF)

    def own(dsts, srcs, devs):
        res = {}
        for way, order in ((0, (H2, H1)), (1, (H1, H2))):
            for n, h in enumerate(order):
                res[(1 - way, n)] = [
                    send(src.at[h], dst.at[1 - way, h], devs[way]) for src, dst in zip(srcs, dsts)
                ]
        return res

    barrier = pltpu.get_barrier_semaphore()
    peers = row + col + tall
    for d in peers:
        pl.semaphore_signal(barrier, inc=1, device_id=d, device_id_type=MESH)
    small = [
        pltpu.make_async_copy(src, dst, list_sem.at[i])
        for i, (src, dst) in enumerate(zip(lists + (mix,), list_v + (mix_in,)))
    ]
    for cp in small:
        cp.start()
    rows = lax.broadcasted_iota(I32, (128, 128), 0)
    lanes = lax.broadcasted_iota(I32, (128, 128), 1)
    wide[...] = jnp.zeros_like(wide)
    for i, cp in enumerate(small[:9]):
        cp.wait()
        wide[i:i + 1, 0:list_v[i].shape[1]] = list_v[i][...].astype(F32)

    def across(i):
        return jnp.broadcast_to(wide[i:i + 1, :], (128, 128))

    def down(i):
        return across(i).T

    def place(owner, first, number, room):
        mine = down(owner)
        same = (mine == across(owner)) & (lanes < rows) & (lanes < number)
        earlier = jnp.sum(jnp.where(same, 1.0, 0.0), axis=1, keepdims=True)
        slot = (mine * room + earlier).astype(I32)
        target = down(first + 2)
        kept = (target.astype(I32) == lanes) & (lanes < 32)
        alive = jnp.sum(jnp.where(kept, across(4), 0.0), axis=1, keepdims=True)
        return slot, (down(first + 1), target, jnp.broadcast_to(alive, (128, 128))), down(first + 3)

    def spread(slot, number, shift, value):
        hit = (slot + shift == lanes) & (rows < number)
        return jnp.sum(jnp.where(hit, value, 0.0), axis=0, keepdims=True)

    slot, parts, coef = place(0, 0, 64, 4)
    tab_i[...] = jnp.zeros_like(tab_i)
    tab_f[...] = jnp.zeros_like(tab_f)
    for r, value in enumerate(parts):
        tab_i[r:r + 1, :] = spread(slot, 64, 0, value).astype(I32)
    tab_f[0:1, :] = spread(slot, 64, 0, coef)
    tab_i[3:4, :] = wide[4:5, :].astype(I32)
    slot, parts, coef = place(5, 5, 16, 8)
    tab_i[4:5, :] = sum(
        spread(slot, 16, 32 * r, value) for r, value in enumerate(parts)
    ).astype(I32)
    tab_f[1:2, :] = spread(slot, 16, 0, coef)
    saves = [
        pltpu.make_async_copy(tab_i, ints, list_sem.at[0]),
        pltpu.make_async_copy(tab_f, flts, list_sem.at[1]),
    ]
    for cp in saves:
        cp.start()
    pl.semaphore_wait(barrier, len(peers))
    for cp in saves:
        cp.wait()
    riders = []
    for k, d in enumerate(row):
        riders.append(send(ints, ints_in.at[back[k]], d))
    for k, d in enumerate(col):
        riders.append(send(ints, ints_in.at[7 + back[k]], d))
        riders.append(send(flts, flts_in.at[back[k]], d))
    for k, d in enumerate(tall):
        riders.append(send(ints, ints_in.at[10 + back[k]], d))
    got_x = own([row_l, row_a], [pno, amp], row)
    got_z = own([z_l], [pno], col)
    got_y = own([y_l, y_a], [pno, amp], tall)
    got_mate = [send(pno, row_l.at[MATE], mate), send(amp, row_a.at[MATE], mate)]
    small[9].wait()
    mix_v[...] = mix_in[...].T

    def metric_of(src, zt):
        def load(i, b):
            return pltpu.make_async_copy(src.at[pl.ds(i * 4, 4)], met_buf.at[b], met_sem.at[b])

        load(0, 0).start()

        def step(i, carry):
            b = i % 2
            load(i, b).wait()

            @pl.when(i < 7)
            def _():
                load(i + 1, 1 - b).start()

            for u in (0, 2):
                two = jnp.concatenate([met_buf[b, u], met_buf[b, u + 1]], axis=1)
                mixed = jnp.dot(mix_v[...], two, preferred_element_type=F32)
                full = (two.astype(F32) + mixed).astype(BF)
                met[zt, i * 4 + u] = full[:, :128].T
                met[zt, i * 4 + u + 1] = full[:, 128:].T
            return carry

        lax.fori_loop(0, 8, step, 0)

    def four(spots, lref, aref, store):
        inters, halves = [], []
        for zt, t, p, live_p, live_q, coef in spots:
            inter = jnp.dot(met[zt, t], lref[p], preferred_element_type=F32)
            ok = (rows < live_p) & (lanes < live_q)
            inters.append(jnp.where(ok, inter, 0.0).astype(BF))
        for (zt, t, p, live_p, live_q, coef), inter in zip(spots, inters):
            halves.append(jnp.dot(inter, aref[p], preferred_element_type=F32).astype(BF))
        for n, (spot, inter, half) in enumerate(zip(spots, inters, halves)):
            term = lax.dot_general(half, inter, (((1,), (1,)), ((), ())), preferred_element_type=F32)
            store(n, (-spot[5] * term).astype(BF))

    def row_slots(j, lref, aref, zt):
        spots = []
        for k in range(4):
            e = row_m[j] * 4 + k
            p = ints_s[7 + zt, 0, e] & 31
            spots.append((zt, ints_s[7 + zt, 1, e] & 31, p, ints_s[7 + zt, 2, e], ints_s[j, 3, p],
                          flts_s[zt, 0, e]))

        def store(n, v):
            terms[zt, j, n] = v

        four(spots, lref, aref, store)

    def row_work(j, lref, aref, first, last):
        def step(zt, carry):
            row_slots(j, lref, aref, zt)
            return carry

        lax.fori_loop(first, last, step, 0)

    def col_work(rel, lref, aref):
        group = (g + (0, 1, 3, 2)[rel]) % 4
        src = OWN if rel == 0 else 10 + rel

        def step(q, carry):
            spots = []
            for n in range(4):
                e = group * 8 + q * 4 + n
                p = ints_s[7, 4, e] & 31
                spots.append((0, ints_s[7, 4, 32 + e] & 31, p, ints_s[7, 4, 64 + e], ints_s[src, 3, p],
                              flts_s[0, 1, e]))

            def store(n, v):
                col_terms[rel, q * 4 + n] = v

            four(spots, lref, aref, store)
            return carry

        lax.fori_loop(0, 2, step, 0)
        keep(col_terms.at[rel], col_out.at[rel])

    passing = {}

    def give(j, zt):
        if zt == 0:
            keep(terms.at[0, j], own_out.at[j])
        elif zt == 3:
            way = 0 if j in PLUS else 1
            passing[j] = send(terms.at[3, j], relay_in.at[j], col[way])
        else:
            send(terms.at[zt, j], terms_in.at[back[zt - 1], j], col[zt - 1])

    def pass_on(j):
        arrive([passing[j]])
        send(relay_in.at[j], terms_in.at[2, j], col[0 if j in PLUS else 1])

    def blocks_of(j):
        if j == OWN:
            return pno, amp
        return row_l.at[j], row_a.at[j]

    def run(stages, late=()):
        def load(i, fn):
            b = i % 2
            for k, (src, dst) in enumerate(zip(stages[i][0], chunks[b])):
                getattr(pltpu.make_async_copy(src, dst, load_sem.at[b, k]), fn)()

        load(0, "start")
        gifts = list(late)
        for i, (blocks, work, after) in enumerate(stages):
            load(i, "wait")
            if i + 1 < len(stages):
                load(i + 1, "start")
            work(*chunks[i % 2])
            for j, zt in gifts:
                give(j, zt)
            gifts = after
        return gifts

    def row_stage(j, first, last):
        return (blocks_of(j), lambda l, a: row_work(j, l, a, first, last),
                [(j, zt) for zt in range(first, last)])

    def col_stage(rel):
        return (y_l.at[rel - 1], y_a.at[rel - 1]), lambda l, a: col_work(rel, l, a), []

    def relay(got, dsts, devs):
        out = []
        for slot, h, way in ((1, H2, 0), (0, H1, 1)):
            arrive(got[(slot, 0)])
            for dst in dsts:
                out.append(send(dst.at[slot, h], dst.at[2, h], devs[way]))
        return out

    metric_of(pno, 0)
    arrive(riders)
    pltpu.sync_copy(ints_in.at[pl.ds(0, 7)], ints_s.at[pl.ds(0, 7)])
    pltpu.sync_copy(ints, ints_s.at[7])
    pltpu.sync_copy(ints_in.at[pl.ds(7, 6)], ints_s.at[pl.ds(8, 6)])
    pltpu.sync_copy(flts, flts_s.at[0])
    pltpu.sync_copy(flts_in, flts_s.at[pl.ds(1, 3)])
    arrive(got_mate)

    def first_work(l, a):
        row_work(OWN, l, a, 0, 1)
        col_work(0, l, a)

    left = run([((pno, amp), first_work, [(OWN, 0)]), row_stage(MATE, 0, 1)])

    far_z = relay(got_z, [z_l], col)
    far_x = []
    for slot, h, way in ((1, H2, 0), (0, H1, 1)):
        arrive(got_x[(slot, 0)])
        for q in (0, 1):
            part = pl.ds((HALF if way == 0 else 0) + q * PIECE, PIECE)
            far_x.append((part, [
                send(row_l.at[slot, part], far_l0.at[part], row[way]),
                send(row_a.at[slot, part], far_a0.at[part], row[way]),
            ]))
    got_mx = []
    for slot, h in ((1, H2), (0, H1)):
        for dst in (row_l, row_a):
            got_mx.append(send(dst.at[slot, h], dst.at[4 + slot, h], mate))
    far_y = relay(got_y, [y_l, y_a], tall)

    for slot in (0, 1):
        arrive(got_z[(slot, 1)])
        metric_of(z_l.at[slot], 1 + slot)
    left = run([row_stage(OWN, 1, 3), row_stage(MATE, 1, 3)], left)
    for slot, h in ((1, H1), (0, H2)):
        arrive(got_x[(slot, 1)])
        for dst in (row_l, row_a):
            got_mx.append(send(dst.at[slot, h], dst.at[4 + slot, h], mate))
    left = run([row_stage(0, 0, 3), row_stage(1, 0, 3)], left)
    arrive(got_mx)
    for slot in (0, 1):
        arrive(got_y[(slot, 1)])
    left = run([row_stage(4, 0, 3), row_stage(5, 0, 3), col_stage(1), col_stage(2)], left)
    arrive(far_z)
    metric_of(z_l.at[2], 3)
    near = (OWN, MATE, 0, 1, 4, 5)
    left = run([row_stage(j, 3, 4) for j in near], left)
    for j in near[:-1]:
        pass_on(j)
    for j, zt in left:
        give(j, zt)
    pass_on(near[-1])

    mate_far = []
    for part, cps in (far_x[0], far_x[2], far_x[1], far_x[3]):
        arrive(cps)
        for src, dst in zip(*far):
            mate_far.append(send(src.at[part], dst.at[part], mate))
    for n, j in ((0, FAR), (1, MATE_FAR)):
        if n == 1:
            arrive(mate_far)
        row_slots(j, *far[n], 3)
        row_slots(j, *far[n], 1)
        give(j, 3)
        row_slots(j, *far[n], 2)
        give(j, 1)
        row_slots(j, *far[n], 0)
        give(j, 2)
    pass_on(FAR)
    give(FAR, 0)
    give(MATE_FAR, 0)
    pass_on(MATE_FAR)
    arrive(far_y)
    run([col_stage(3)])
    for cp in local:
        cp.wait()
    for cp in live:
        cp.wait_send()
        if id(cp) not in arrived:
            cp.wait_recv()


def main(pno, amp, mix, lists):
    any_spec = pl.BlockSpec(memory_space=pl.ANY)
    shape = jax.ShapeDtypeStruct
    outs = [
        shape((8, 4, 128, 128), BF),
        shape((4, 8, 128, 128), BF),
        shape((3, 8, 4, 128, 128), BF),
        shape((8, 128), I32),
        shape((8, 128), F32),
        shape((8, 4, 128, 128), BF),
        shape((7, 32, 512, 128), BF),
        shape((7, 32, 128, 128), BF),
        shape((3, 32, 512, 128), BF),
        shape((3, 32, 512, 128), BF),
        shape((3, 32, 128, 128), BF),
        shape((13, 8, 128), I32),
        shape((3, 8, 128), F32),
    ]
    return pl.pallas_call(
        main_kernel,
        out_shape=outs,
        in_specs=[any_spec] * 12,
        out_specs=[any_spec] * len(outs),
        scratch_shapes=[pltpu.VMEM(v.shape, v.dtype) for v in lists] + [
            pltpu.VMEM((16, 128), F32),
            pltpu.VMEM((8, 128), I32),
            pltpu.VMEM((8, 128), F32),
            pltpu.VMEM((512, 512), BF),
            pltpu.VMEM((512, 512), BF),
            pltpu.VMEM((4, 32, 128, 512), BF),
            pltpu.VMEM((32, 512, 128), BF),
            pltpu.VMEM((32, 512, 128), BF),
            pltpu.VMEM((32, 128, 128), BF),
            pltpu.VMEM((32, 128, 128), BF),
            pltpu.VMEM((32, 512, 128), BF),
            pltpu.VMEM((32, 512, 128), BF),
            pltpu.VMEM((32, 128, 128), BF),
            pltpu.VMEM((32, 128, 128), BF),
            pltpu.VMEM((4, 8, 4, 128, 128), BF),
            pltpu.VMEM((4, 8, 128, 128), BF),
            pltpu.VMEM((2, 4, 512, 128), BF),
            pltpu.SMEM((14, 8, 128), I32),
            pltpu.SMEM((4, 8, 128), F32),
            pltpu.SemaphoreType.DMA((128,)),
            pltpu.SemaphoreType.DMA((128,)),
            pltpu.SemaphoreType.DMA((2, 2)),
            pltpu.SemaphoreType.DMA((2,)),
            pltpu.SemaphoreType.DMA((16,)),
            pltpu.SemaphoreType.DMA((10,)),
        ],
        compiler_params=pltpu.CompilerParams(
            collective_id=0, has_side_effects=True, vmem_limit_bytes=63 << 20
        ),
    )(pno, amp, mix, *lists)


def sum_kernel(ints, own_terms, col_terms, terms_in, out, own_v, col_v, in_v, sem):
    me = lax.axis_index("mem")
    g = lax.axis_index("grp")
    core = me % 2
    z = (me // 2) % 4
    x = me // 8
    loads = [
        pltpu.make_async_copy(own_terms, own_v, sem.at[0]),
        pltpu.make_async_copy(col_terms, col_v, sem.at[1]),
    ] + [pltpu.make_async_copy(terms_in.at[i], in_v.at[i], sem.at[2 + i]) for i in range(3)]
    for cp in loads:
        cp.start()
    out[...] = jnp.zeros_like(out)
    from_z = (0, 1, 3, 2)
    from_x = (1, 3, 2, 0, 1, 3, 2, 0)
    for zi in range(4):
        loads[zi + 1 if zi else 0].wait()
        for j in range(8):
            m = ((x + from_x[j]) % 4) * 8 + ((z + from_z[zi]) % 4) * 2 + (core + (3 <= j < 7)) % 2
            for k in range(4):
                e = m * 4 + k

                @pl.when(ints[2, e] > 0)
                def _():
                    t = ints[1, e]
                    v = own_v[j, k] if zi == 0 else in_v[zi - 1, j, k]
                    out[t] = out[t] + v.astype(F32)

        if zi == 0:
            loads[1].wait()
            for rel in range(4):
                for k in range(8):
                    e = ((g + (0, 1, 3, 2)[rel]) % 4) * 8 + k

                    @pl.when(ints[4, 64 + e] > 0)
                    def _():
                        t = ints[4, 32 + e]
                        out[t] = out[t] + col_v[rel, k].astype(F32)


def total(ints, own_terms, col_terms, terms_in):
    any_spec = pl.BlockSpec(memory_space=pl.ANY)
    return pl.pallas_call(
        sum_kernel,
        out_shape=jax.ShapeDtypeStruct((32, 128, 128), F32),
        in_specs=[pl.BlockSpec(memory_space=pltpu.SMEM)] + [any_spec] * 3,
        out_specs=pl.BlockSpec(memory_space=pltpu.VMEM),
        scratch_shapes=[
            pltpu.VMEM(own_terms.shape, BF),
            pltpu.VMEM(col_terms.shape, BF),
            pltpu.VMEM(terms_in.shape, BF),
            pltpu.SemaphoreType.DMA((5,)),
        ],
        compiler_params=pltpu.CompilerParams(vmem_limit_bytes=63 << 20),
    )(ints, own_terms, col_terms, terms_in)


def shards(
    pno, amplitudes, pno_count, pao_coupling,
    row_owner, row_pair, row_target, row_coef,
    column_owner, column_pair, column_target, column_coef,
):
    lists = [
        v.reshape(1, -1)
        for v in (
            row_owner, row_pair, row_target, row_coef, pno_count,
            column_owner, column_pair, column_target, column_coef,
        )
    ]
    own_terms, col_terms, terms_in, ints = main(pno, amplitudes, pao_coupling, lists)[:4]
    return total(ints, own_terms, col_terms, terms_in)


def solution(mesh):
    both = P(("grp", "mem"))
    in_specs = (
        P(("grp", "mem"), None, None),
        P(("grp", "mem"), None, None),
        both,
        P(),
        P(("grp", "mem"), None),
        both,
        both,
        both,
        P(("grp", "mem"), None),
        both,
        both,
        both,
    )
    out_specs = P(("grp", "mem"), None, None)
    return jax.shard_map(shards, mesh=mesh, in_specs=in_specs, out_specs=out_specs, check_vma=False)
```

```python
import jax
import jax.numpy as jnp
from jax import lax
from jax.experimental import pallas as pl
from jax.experimental.pallas import tpu as pltpu
from jax.sharding import PartitionSpec as P

MESH = pl.DeviceIdType.MESH
BF = jnp.bfloat16
F32 = jnp.float32
I32 = jnp.int32
HALF = 16
PIECE = 8
MATE = 3
FAR, MATE_FAR = 2, 6
OWN = 7
PLUS = (0, 2, 3, 4)


def main_kernel(
    pno, amp, mix, *refs,
):
    lists = refs[:9]
    (
        own_out, col_out, terms_in, ints, flts,
        relay_in, row_l, row_a, z_l, y_l, y_a, ints_in, flts_in,
    ) = refs[9:22]
    list_v = refs[22:31]
    (
        wide, tab_i, tab_f, mix_in, mix_v, met,
        own_l, own_a, mate_l, mate_a, chunk_l0, chunk_l1, chunk_a0, chunk_a1, far_l0, far_l1, far_a0, far_a1,
        terms, col_terms, met_buf, ints_s, flts_s, send_sem, recv_sem, load_sem, met_sem,
        out_sem, list_sem,
    ) = refs[31:]
    chunks = ((chunk_l0, chunk_a0), (chunk_l1, chunk_a1))
    far = ((far_l0, far_a0), (far_l1, far_a1))
    me = lax.axis_index("mem")
    g = lax.axis_index("grp")
    core = me % 2
    z = (me // 2) % 4
    x = me // 8

    def member(dx, dz, dc):
        return ((x + dx) % 4) * 8 + ((z + dz) % 4) * 2 + (core + dc) % 2

    def up(dg):
        return ((g + dg) % 4, me)

    row_m = [member(1, 0, 0), member(3, 0, 0), member(2, 0, 0), member(0, 0, 1),
             member(1, 0, 1), member(3, 0, 1), member(2, 0, 1), me]
    row = [(g, m) for m in row_m[:7]]
    col = [(g, member(0, d, 0)) for d in (1, 3, 2)]
    tall = [up(1), up(3), up(2)]
    back = (1, 0, 2, 3, 5, 4, 6)
    mate = row[MATE]

    live = []
    arrived = set()

    def send(src, dst, dev):
        i = len(live)
        cp = pltpu.make_async_remote_copy(
            src_ref=src, dst_ref=dst, send_sem=send_sem.at[i], recv_sem=recv_sem.at[i],
            device_id=dev, device_id_type=MESH,
        )
        cp.start()
        live.append(cp)
        return cp

    def arrive(cps):
        for cp in cps:
            cp.wait_recv()
            arrived.add(id(cp))

    local = []

    def keep(src, dst):
        cp = pltpu.make_async_copy(src, dst, out_sem.at[len(local)])
        cp.start()
        local.append(cp)

    H1 = pl.ds(0, HALF)
    H2 = pl.ds(HALF, HALF)

    def own(dsts, srcs, devs):
        res = {}
        for way, order in ((0, (H2, H1)), (1, (H1, H2))):
            for n, h in enumerate(order):
                res[(1 - way, n)] = [
                    send(src.at[h], dst.at[1 - way, h], devs[way]) for src, dst in zip(srcs, dsts)
                ]
        return res

    barrier = pltpu.get_barrier_semaphore()
    peers = row + col + tall
    for d in peers:
        pl.semaphore_signal(barrier, inc=1, device_id=d, device_id_type=MESH)
    small = [
        pltpu.make_async_copy(src, dst, list_sem.at[i])
        for i, (src, dst) in enumerate(zip(lists + (mix,), list_v + (mix_in,)))
    ]
    for cp in small:
        cp.start()
    rows = lax.broadcasted_iota(I32, (128, 128), 0)
    lanes = lax.broadcasted_iota(I32, (128, 128), 1)
    wide[...] = jnp.zeros_like(wide)
    for i, cp in enumerate(small[:9]):
        cp.wait()
        wide[i:i + 1, 0:list_v[i].shape[1]] = list_v[i][...].astype(F32)

    def across(i):
        return jnp.broadcast_to(wide[i:i + 1, :], (128, 128))

    def down(i):
        return across(i).T

    def place(owner, first, number, room):
        mine = down(owner)
        same = (mine == across(owner)) & (lanes < rows) & (lanes < number)
        earlier = jnp.sum(jnp.where(same, 1.0, 0.0), axis=1, keepdims=True)
        slot = (mine * room + earlier).astype(I32)
        target = down(first + 2)
        kept = (target.astype(I32) == lanes) & (lanes < 32)
        alive = jnp.sum(jnp.where(kept, across(4), 0.0), axis=1, keepdims=True)
        return slot, (down(first + 1), target, jnp.broadcast_to(alive, (128, 128))), down(first + 3)

    def spread(slot, number, shift, value):
        hit = (slot + shift == lanes) & (rows < number)
        return jnp.sum(jnp.where(hit, value, 0.0), axis=0, keepdims=True)

    slot, parts, coef = place(0, 0, 64, 4)
    tab_i[...] = jnp.zeros_like(tab_i)
    tab_f[...] = jnp.zeros_like(tab_f)
    for r, value in enumerate(parts):
        tab_i[r:r + 1, :] = spread(slot, 64, 0, value).astype(I32)
    tab_f[0:1, :] = spread(slot, 64, 0, coef)
    tab_i[3:4, :] = wide[4:5, :].astype(I32)
    slot, parts, coef = place(5, 5, 16, 8)
    tab_i[4:5, :] = sum(
        spread(slot, 16, 32 * r, value) for r, value in enumerate(parts)
    ).astype(I32)
    tab_f[1:2, :] = spread(slot, 16, 0, coef)
    saves = [
        pltpu.make_async_copy(tab_i, ints, list_sem.at[0]),
        pltpu.make_async_copy(tab_f, flts, list_sem.at[1]),
    ]
    for cp in saves:
        cp.start()
    pl.semaphore_wait(barrier, len(peers))
    for cp in saves:
        cp.wait()
    riders = []
    for k, d in enumerate(row):
        riders.append(send(ints, ints_in.at[back[k]], d))
    for k, d in enumerate(col):
        riders.append(send(ints, ints_in.at[7 + back[k]], d))
        riders.append(send(flts, flts_in.at[back[k]], d))
    for k, d in enumerate(tall):
        riders.append(send(ints, ints_in.at[10 + back[k]], d))
    got_x = own([row_l, row_a], [pno, amp], row)
    got_z = own([z_l], [pno], col)
    got_y = own([y_l, y_a], [pno, amp], tall)
    got_mate = [send(pno, mate_l, mate), send(amp, mate_a, mate)]
    home = [
        pltpu.make_async_copy(pno, own_l, list_sem.at[2]),
        pltpu.make_async_copy(amp, own_a, list_sem.at[3]),
    ]
    for cp in home:
        cp.start()
    small[9].wait()
    mix_v[...] = mix_in[...].T

    def metric_of(src, zt):
        def load(i, b):
            return pltpu.make_async_copy(src.at[pl.ds(i * 4, 4)], met_buf.at[b], met_sem.at[b])

        load(0, 0).start()

        def step(i, carry):
            b = i % 2
            load(i, b).wait()

            @pl.when(i < 7)
            def _():
                load(i + 1, 1 - b).start()

            for u in (0, 2):
                two = jnp.concatenate([met_buf[b, u], met_buf[b, u + 1]], axis=1)
                mixed = jnp.dot(mix_v[...], two, preferred_element_type=F32)
                full = (two.astype(F32) + mixed).astype(BF)
                met[zt, i * 4 + u] = full[:, :128].T
                met[zt, i * 4 + u + 1] = full[:, 128:].T
            return carry

        lax.fori_loop(0, 8, step, 0)

    def four(spots, lref, aref, store):
        inters, halves = [], []
        for zt, t, p, live_p, live_q, coef in spots:
            inter = jnp.dot(met[zt, t], lref[p], preferred_element_type=F32)
            ok = (rows < live_p) & (lanes < live_q)
            inters.append(jnp.where(ok, inter, 0.0).astype(BF))
        for (zt, t, p, live_p, live_q, coef), inter in zip(spots, inters):
            halves.append(jnp.dot(inter, aref[p], preferred_element_type=F32).astype(BF))
        for n, (spot, inter, half) in enumerate(zip(spots, inters, halves)):
            term = lax.dot_general(half, inter, (((1,), (1,)), ((), ())), preferred_element_type=F32)
            store(n, (-spot[5] * term).astype(BF))

    def row_slots(j, lref, aref, zt):
        spots = []
        for k in range(4):
            e = row_m[j] * 4 + k
            p = ints_s[7 + zt, 0, e] & 31
            spots.append((zt, ints_s[7 + zt, 1, e] & 31, p, ints_s[7 + zt, 2, e], ints_s[j, 3, p],
                          flts_s[zt, 0, e]))

        def store(n, v):
            terms[zt, j, n] = v

        four(spots, lref, aref, store)

    def row_work(j, lref, aref, first, last):
        def step(zt, carry):
            row_slots(j, lref, aref, zt)
            return carry

        lax.fori_loop(first, last, step, 0)

    def col_work(rel, lref, aref):
        group = (g + (0, 1, 3, 2)[rel]) % 4
        src = OWN if rel == 0 else 10 + rel

        def step(q, carry):
            spots = []
            for n in range(4):
                e = group * 8 + q * 4 + n
                p = ints_s[7, 4, e] & 31
                spots.append((0, ints_s[7, 4, 32 + e] & 31, p, ints_s[7, 4, 64 + e], ints_s[src, 3, p],
                              flts_s[0, 1, e]))

            def store(n, v):
                col_terms[rel, q * 4 + n] = v

            four(spots, lref, aref, store)
            return carry

        lax.fori_loop(0, 2, step, 0)
        keep(col_terms.at[rel], col_out.at[rel])

    passing = {}

    def give(j, zt):
        if zt == 0:
            keep(terms.at[0, j], own_out.at[j])
        elif zt == 3:
            way = 0 if j in PLUS else 1
            passing[j] = send(terms.at[3, j], relay_in.at[j], col[way])
        else:
            send(terms.at[zt, j], terms_in.at[back[zt - 1], j], col[zt - 1])

    def pass_on(j):
        arrive([passing[j]])
        send(relay_in.at[j], terms_in.at[2, j], col[0 if j in PLUS else 1])

    def blocks_of(j):
        if j in (OWN, MATE):
            return None
        return row_l.at[j], row_a.at[j]

    def run(stages, late=()):
        loads = [n for n, stage in enumerate(stages) if stage[0] is not None]

        def load(i, fn):
            b = i % 2
            for k, (src, dst) in enumerate(zip(stages[loads[i]][0], chunks[b])):
                getattr(pltpu.make_async_copy(src, dst, load_sem.at[b, k]), fn)()

        if loads:
            load(0, "start")
        gifts = list(late)
        for n, (blocks, work, after) in enumerate(stages):
            if blocks is None:
                work(None, None)
            else:
                i = loads.index(n)
                load(i, "wait")
                if i + 1 < len(loads):
                    load(i + 1, "start")
                work(*chunks[i % 2])
            for j, zt in gifts:
                give(j, zt)
            gifts = after
        return gifts

    stay = {OWN: (own_l, own_a), MATE: (mate_l, mate_a)}

    def row_stage(j, first, last):
        return (blocks_of(j), lambda l, a: row_work(j, *stay.get(j, (l, a)), first, last),
                [(j, zt) for zt in range(first, last)])

    def col_stage(rel):
        return (y_l.at[rel - 1], y_a.at[rel - 1]), lambda l, a: col_work(rel, l, a), []

    def relay(got, dsts, devs):
        out = []
        for slot, h, way in ((1, H2, 0), (0, H1, 1)):
            arrive(got[(slot, 0)])
            for dst in dsts:
                out.append(send(dst.at[slot, h], dst.at[2, h], devs[way]))
        return out

    metric_of(pno, 0)
    arrive(riders)
    pltpu.sync_copy(ints_in.at[pl.ds(0, 7)], ints_s.at[pl.ds(0, 7)])
    pltpu.sync_copy(ints, ints_s.at[7])
    pltpu.sync_copy(ints_in.at[pl.ds(7, 6)], ints_s.at[pl.ds(8, 6)])
    pltpu.sync_copy(flts, flts_s.at[0])
    pltpu.sync_copy(flts_in, flts_s.at[pl.ds(1, 3)])
    arrive(got_mate)

    def first_work(l, a):
        row_work(OWN, own_l, own_a, 0, 1)
        col_work(0, own_l, own_a)

    for cp in home:
        cp.wait()

    left = run([(None, first_work, [(OWN, 0)]), row_stage(MATE, 0, 1)])

    far_z = relay(got_z, [z_l], col)
    far_x = []
    for slot, h, way in ((1, H2, 0), (0, H1, 1)):
        arrive(got_x[(slot, 0)])
        for q in (0, 1):
            part = pl.ds((HALF if way == 0 else 0) + q * PIECE, PIECE)
            far_x.append((part, [
                send(row_l.at[slot, part], far_l0.at[part], row[way]),
                send(row_a.at[slot, part], far_a0.at[part], row[way]),
            ]))
    got_mx = []
    for slot, h in ((1, H2), (0, H1)):
        for dst in (row_l, row_a):
            got_mx.append(send(dst.at[slot, h], dst.at[4 + slot, h], mate))
    far_y = relay(got_y, [y_l, y_a], tall)

    for slot in (0, 1):
        arrive(got_z[(slot, 1)])
        metric_of(z_l.at[slot], 1 + slot)
    left = run([row_stage(OWN, 1, 3), row_stage(MATE, 1, 3)], left)
    for slot, h in ((1, H1), (0, H2)):
        arrive(got_x[(slot, 1)])
        for dst in (row_l, row_a):
            got_mx.append(send(dst.at[slot, h], dst.at[4 + slot, h], mate))
    left = run([row_stage(0, 0, 3), row_stage(1, 0, 3)], left)
    arrive(got_mx)
    for slot in (0, 1):
        arrive(got_y[(slot, 1)])
    left = run([row_stage(4, 0, 3), row_stage(5, 0, 3), col_stage(1), col_stage(2)], left)
    arrive(far_z)
    metric_of(z_l.at[2], 3)
    near = (OWN, MATE, 0, 1, 4, 5)
    left = run([row_stage(j, 3, 4) for j in near], left)
    for j in near[:-1]:
        pass_on(j)
    for j, zt in left:
        give(j, zt)
    pass_on(near[-1])

    mate_far = []
    for part, cps in (far_x[0], far_x[2], far_x[1], far_x[3]):
        arrive(cps)
        for src, dst in zip(*far):
            mate_far.append(send(src.at[part], dst.at[part], mate))
    for n, j in ((0, FAR), (1, MATE_FAR)):
        if n == 1:
            arrive(mate_far)
        row_slots(j, *far[n], 3)
        row_slots(j, *far[n], 1)
        give(j, 3)
        row_slots(j, *far[n], 2)
        give(j, 1)
        row_slots(j, *far[n], 0)
        give(j, 2)
    pass_on(FAR)
    give(FAR, 0)
    give(MATE_FAR, 0)
    pass_on(MATE_FAR)
    arrive(far_y)
    run([col_stage(3)])
    for cp in local:
        cp.wait()
    for cp in live:
        cp.wait_send()
        if id(cp) not in arrived:
            cp.wait_recv()


def main(pno, amp, mix, lists):
    any_spec = pl.BlockSpec(memory_space=pl.ANY)
    shape = jax.ShapeDtypeStruct
    outs = [
        shape((8, 4, 128, 128), BF),
        shape((4, 8, 128, 128), BF),
        shape((3, 8, 4, 128, 128), BF),
        shape((8, 128), I32),
        shape((8, 128), F32),
        shape((8, 4, 128, 128), BF),
        shape((7, 32, 512, 128), BF),
        shape((7, 32, 128, 128), BF),
        shape((3, 32, 512, 128), BF),
        shape((3, 32, 512, 128), BF),
        shape((3, 32, 128, 128), BF),
        shape((13, 8, 128), I32),
        shape((3, 8, 128), F32),
    ]
    return pl.pallas_call(
        main_kernel,
        out_shape=outs,
        in_specs=[any_spec] * 12,
        out_specs=[any_spec] * len(outs),
        scratch_shapes=[pltpu.VMEM(v.shape, v.dtype) for v in lists] + [
            pltpu.VMEM((16, 128), F32),
            pltpu.VMEM((8, 128), I32),
            pltpu.VMEM((8, 128), F32),
            pltpu.VMEM((512, 512), BF),
            pltpu.VMEM((512, 512), BF),
            pltpu.VMEM((4, 32, 128, 512), BF),
            pltpu.VMEM((32, 512, 128), BF),
            pltpu.VMEM((32, 128, 128), BF),
            pltpu.VMEM((32, 512, 128), BF),
            pltpu.VMEM((32, 128, 128), BF),
            pltpu.VMEM((32, 512, 128), BF),
            pltpu.VMEM((32, 512, 128), BF),
            pltpu.VMEM((32, 128, 128), BF),
            pltpu.VMEM((32, 128, 128), BF),
            pltpu.VMEM((32, 512, 128), BF),
            pltpu.VMEM((32, 512, 128), BF),
            pltpu.VMEM((32, 128, 128), BF),
            pltpu.VMEM((32, 128, 128), BF),
            pltpu.VMEM((4, 8, 4, 128, 128), BF),
            pltpu.VMEM((4, 8, 128, 128), BF),
            pltpu.VMEM((2, 4, 512, 128), BF),
            pltpu.SMEM((14, 8, 128), I32),
            pltpu.SMEM((4, 8, 128), F32),
            pltpu.SemaphoreType.DMA((128,)),
            pltpu.SemaphoreType.DMA((128,)),
            pltpu.SemaphoreType.DMA((2, 2)),
            pltpu.SemaphoreType.DMA((2,)),
            pltpu.SemaphoreType.DMA((16,)),
            pltpu.SemaphoreType.DMA((10,)),
        ],
        compiler_params=pltpu.CompilerParams(
            collective_id=0, has_side_effects=True, vmem_limit_bytes=63 << 20
        ),
    )(pno, amp, mix, *lists)


def sum_kernel(ints, own_terms, col_terms, terms_in, out, own_v, col_v, in_v, sem):
    me = lax.axis_index("mem")
    g = lax.axis_index("grp")
    core = me % 2
    z = (me // 2) % 4
    x = me // 8
    loads = [
        pltpu.make_async_copy(own_terms, own_v, sem.at[0]),
        pltpu.make_async_copy(col_terms, col_v, sem.at[1]),
    ] + [pltpu.make_async_copy(terms_in.at[i], in_v.at[i], sem.at[2 + i]) for i in range(3)]
    for cp in loads:
        cp.start()
    out[...] = jnp.zeros_like(out)
    from_z = (0, 1, 3, 2)
    from_x = (1, 3, 2, 0, 1, 3, 2, 0)
    for zi in range(4):
        loads[zi + 1 if zi else 0].wait()
        for j in range(8):
            m = ((x + from_x[j]) % 4) * 8 + ((z + from_z[zi]) % 4) * 2 + (core + (3 <= j < 7)) % 2
            for k in range(4):
                e = m * 4 + k

                @pl.when(ints[2, e] > 0)
                def _():
                    t = ints[1, e]
                    v = own_v[j, k] if zi == 0 else in_v[zi - 1, j, k]
                    out[t] = out[t] + v.astype(F32)

        if zi == 0:
            loads[1].wait()
            for rel in range(4):
                for k in range(8):
                    e = ((g + (0, 1, 3, 2)[rel]) % 4) * 8 + k

                    @pl.when(ints[4, 64 + e] > 0)
                    def _():
                        t = ints[4, 32 + e]
                        out[t] = out[t] + col_v[rel, k].astype(F32)


def total(ints, own_terms, col_terms, terms_in):
    any_spec = pl.BlockSpec(memory_space=pl.ANY)
    return pl.pallas_call(
        sum_kernel,
        out_shape=jax.ShapeDtypeStruct((32, 128, 128), F32),
        in_specs=[pl.BlockSpec(memory_space=pltpu.SMEM)] + [any_spec] * 3,
        out_specs=pl.BlockSpec(memory_space=pltpu.VMEM),
        scratch_shapes=[
            pltpu.VMEM(own_terms.shape, BF),
            pltpu.VMEM(col_terms.shape, BF),
            pltpu.VMEM(terms_in.shape, BF),
            pltpu.SemaphoreType.DMA((5,)),
        ],
        compiler_params=pltpu.CompilerParams(vmem_limit_bytes=63 << 20),
    )(ints, own_terms, col_terms, terms_in)


def shards(
    pno, amplitudes, pno_count, pao_coupling,
    row_owner, row_pair, row_target, row_coef,
    column_owner, column_pair, column_target, column_coef,
):
    lists = [
        v.reshape(1, -1)
        for v in (
            row_owner, row_pair, row_target, row_coef, pno_count,
            column_owner, column_pair, column_target, column_coef,
        )
    ]
    own_terms, col_terms, terms_in, ints = main(pno, amplitudes, pao_coupling, lists)[:4]
    return total(ints, own_terms, col_terms, terms_in)


def solution(mesh):
    both = P(("grp", "mem"))
    in_specs = (
        P(("grp", "mem"), None, None),
        P(("grp", "mem"), None, None),
        both,
        P(),
        P(("grp", "mem"), None),
        both,
        both,
        both,
        P(("grp", "mem"), None),
        both,
        both,
        both,
    )
    out_specs = P(("grp", "mem"), None, None)
    return jax.shard_map(shards, mesh=mesh, in_specs=in_specs, out_specs=out_specs, check_vma=False)
```

```python
import jax
import jax.numpy as jnp
from jax import lax
from jax.experimental import pallas as pl
from jax.experimental.pallas import tpu as pltpu
from jax.sharding import PartitionSpec as P

MESH = pl.DeviceIdType.MESH
BF = jnp.bfloat16
F32 = jnp.float32
I32 = jnp.int32
HALF = 16
PIECE = 8
MATE = 3
FAR, MATE_FAR = 2, 6
OWN = 7
PLUS = (0, 2, 3, 4)


def main_kernel(
    pno, amp, mix, *refs,
):
    lists = refs[:9]
    (
        own_out, col_out, terms_in, ints, flts,
        relay_in, row_l, row_a, z_l, y_l, y_a, ints_in, flts_in,
    ) = refs[9:22]
    list_v = refs[22:31]
    (
        wide, tab_i, tab_f, mix_in, mix_v, met,
        own_l, own_a, mate_l, mate_a, chunk_l0, chunk_l1, chunk_a0, chunk_a1, far_l0, far_l1, far_a0, far_a1,
        terms, col_terms, met_buf, ints_s, flts_s, send_sem, recv_sem, load_sem, met_sem,
        out_sem, list_sem,
    ) = refs[31:]
    chunks = ((chunk_l0, chunk_a0), (chunk_l1, chunk_a1))
    far = ((far_l0, far_a0), (far_l1, far_a1))
    me = lax.axis_index("mem")
    g = lax.axis_index("grp")
    core = me % 2
    z = (me // 2) % 4
    x = me // 8

    def member(dx, dz, dc):
        return ((x + dx) % 4) * 8 + ((z + dz) % 4) * 2 + (core + dc) % 2

    def up(dg):
        return ((g + dg) % 4, me)

    row_m = [member(1, 0, 0), member(3, 0, 0), member(2, 0, 0), member(0, 0, 1),
             member(1, 0, 1), member(3, 0, 1), member(2, 0, 1), me]
    row = [(g, m) for m in row_m[:7]]
    col = [(g, member(0, d, 0)) for d in (1, 3, 2)]
    tall = [up(1), up(3), up(2)]
    back = (1, 0, 2, 3, 5, 4, 6)
    mate = row[MATE]

    live = []
    arrived = set()

    def send(src, dst, dev):
        i = len(live)
        cp = pltpu.make_async_remote_copy(
            src_ref=src, dst_ref=dst, send_sem=send_sem.at[i], recv_sem=recv_sem.at[i],
            device_id=dev, device_id_type=MESH,
        )
        cp.start()
        live.append(cp)
        return cp

    def arrive(cps):
        for cp in cps:
            cp.wait_recv()
            arrived.add(id(cp))

    local = []

    def keep(src, dst):
        cp = pltpu.make_async_copy(src, dst, out_sem.at[len(local)])
        cp.start()
        local.append(cp)

    H1 = pl.ds(0, HALF)
    H2 = pl.ds(HALF, HALF)

    def own(dsts, srcs, devs):
        res = {}
        for way, order in ((0, (H2, H1)), (1, (H1, H2))):
            for n, h in enumerate(order):
                res[(1 - way, n)] = [
                    send(src.at[h], dst.at[1 - way, h], devs[way]) for src, dst in zip(srcs, dsts)
                ]
        return res

    barrier = pltpu.get_barrier_semaphore()
    peers = row + col + tall
    for d in peers:
        pl.semaphore_signal(barrier, inc=1, device_id=d, device_id_type=MESH)
    small = [
        pltpu.make_async_copy(src, dst, list_sem.at[i])
        for i, (src, dst) in enumerate(zip(lists + (mix,), list_v + (mix_in,)))
    ]
    for cp in small:
        cp.start()
    rows = lax.broadcasted_iota(I32, (128, 128), 0)
    lanes = lax.broadcasted_iota(I32, (128, 128), 1)
    wide[...] = jnp.zeros_like(wide)
    for i, cp in enumerate(small[:9]):
        cp.wait()
        wide[i:i + 1, 0:list_v[i].shape[1]] = list_v[i][...].astype(F32)

    def across(i):
        return jnp.broadcast_to(wide[i:i + 1, :], (128, 128))

    def down(i):
        return across(i).T

    def place(owner, first, number, room):
        mine = down(owner)
        same = (mine == across(owner)) & (lanes < rows) & (lanes < number)
        earlier = jnp.sum(jnp.where(same, 1.0, 0.0), axis=1, keepdims=True)
        slot = (mine * room + earlier).astype(I32)
        target = down(first + 2)
        kept = (target.astype(I32) == lanes) & (lanes < 32)
        alive = jnp.sum(jnp.where(kept, across(4), 0.0), axis=1, keepdims=True)
        return slot, (down(first + 1), target, jnp.broadcast_to(alive, (128, 128))), down(first + 3)

    def spread(slot, number, shift, value):
        hit = (slot + shift == lanes) & (rows < number)
        return jnp.sum(jnp.where(hit, value, 0.0), axis=0, keepdims=True)

    slot, parts, coef = place(0, 0, 64, 4)
    tab_i[...] = jnp.zeros_like(tab_i)
    tab_f[...] = jnp.zeros_like(tab_f)
    for r, value in enumerate(parts):
        tab_i[r:r + 1, :] = spread(slot, 64, 0, value).astype(I32)
    tab_f[0:1, :] = spread(slot, 64, 0, coef)
    tab_i[3:4, :] = wide[4:5, :].astype(I32)
    slot, parts, coef = place(5, 5, 16, 8)
    tab_i[4:5, :] = sum(
        spread(slot, 16, 32 * r, value) for r, value in enumerate(parts)
    ).astype(I32)
    tab_f[1:2, :] = spread(slot, 16, 0, coef)
    saves = [
        pltpu.make_async_copy(tab_i, ints, list_sem.at[0]),
        pltpu.make_async_copy(tab_f, flts, list_sem.at[1]),
    ]
    for cp in saves:
        cp.start()
    pl.semaphore_wait(barrier, len(peers))
    for cp in saves:
        cp.wait()
    riders = []
    for k, d in enumerate(row):
        riders.append(send(ints, ints_in.at[back[k]], d))
    for k, d in enumerate(col):
        riders.append(send(ints, ints_in.at[7 + back[k]], d))
        riders.append(send(flts, flts_in.at[back[k]], d))
    for k, d in enumerate(tall):
        riders.append(send(ints, ints_in.at[10 + back[k]], d))
    got_x = own([row_l, row_a], [pno, amp], row)
    got_z = own([z_l], [pno], col)
    got_y = own([y_l, y_a], [pno, amp], tall)
    got_mate = [send(pno, mate_l, mate), send(amp, mate_a, mate)]
    home = [
        pltpu.make_async_copy(pno, own_l, list_sem.at[2]),
        pltpu.make_async_copy(amp, own_a, list_sem.at[3]),
    ]
    for cp in home:
        cp.start()
    small[9].wait()
    mix_v[...] = mix_in[...].T

    def metric_of(src, zt):
        def load(i, b):
            return pltpu.make_async_copy(src.at[pl.ds(i * 4, 4)], met_buf.at[b], met_sem.at[b])

        load(0, 0).start()

        def step(i, carry):
            b = i % 2
            load(i, b).wait()

            @pl.when(i < 7)
            def _():
                load(i + 1, 1 - b).start()

            for u in (0, 2):
                two = jnp.concatenate([met_buf[b, u], met_buf[b, u + 1]], axis=1)
                mixed = jnp.dot(mix_v[...], two, preferred_element_type=F32)
                full = (two.astype(F32) + mixed).astype(BF)
                met[zt, i * 4 + u] = full[:, :128].T
                met[zt, i * 4 + u + 1] = full[:, 128:].T
            return carry

        lax.fori_loop(0, 8, step, 0)

    def four(spots, lref, aref, store):
        inters, halves = [], []
        for zt, t, p, live_p, live_q, coef in spots:
            inter = jnp.dot(met[zt, t], lref[p], preferred_element_type=F32)
            ok = (rows < live_p) & (lanes < live_q)
            inters.append(jnp.where(ok, inter, 0.0).astype(BF))
        for (zt, t, p, live_p, live_q, coef), inter in zip(spots, inters):
            halves.append(jnp.dot(inter, aref[p], preferred_element_type=F32).astype(BF))
        for n, (spot, inter, half) in enumerate(zip(spots, inters, halves)):
            term = lax.dot_general(half, inter, (((1,), (1,)), ((), ())), preferred_element_type=F32)
            store(n, (-spot[5] * term).astype(BF))

    def row_slots(j, lref, aref, zt):
        spots = []
        for k in range(4):
            e = row_m[j] * 4 + k
            p = ints_s[7 + zt, 0, e] & 31
            spots.append((zt, ints_s[7 + zt, 1, e] & 31, p, ints_s[7 + zt, 2, e], ints_s[j, 3, p],
                          flts_s[zt, 0, e]))

        def store(n, v):
            terms[zt, j, n] = v

        four(spots, lref, aref, store)

    def row_work(j, lref, aref, first, last):
        def step(zt, carry):
            row_slots(j, lref, aref, zt)
            return carry

        lax.fori_loop(first, last, step, 0)

    def col_work(rel, lref, aref):
        group = (g + (0, 1, 3, 2)[rel]) % 4
        src = OWN if rel == 0 else 10 + rel

        def step(q, carry):
            spots = []
            for n in range(4):
                e = group * 8 + q * 4 + n
                p = ints_s[7, 4, e] & 31
                spots.append((0, ints_s[7, 4, 32 + e] & 31, p, ints_s[7, 4, 64 + e], ints_s[src, 3, p],
                              flts_s[0, 1, e]))

            def store(n, v):
                col_terms[rel, q * 4 + n] = v

            four(spots, lref, aref, store)
            return carry

        lax.fori_loop(0, 2, step, 0)
        keep(col_terms.at[rel], col_out.at[rel])

    passing = {}

    def give(j, zt):
        if zt == 0:
            keep(terms.at[0, j], own_out.at[j])
        elif zt == 3:
            way = 0 if j in PLUS else 1
            passing[j] = send(terms.at[3, j], relay_in.at[j], col[way])
        else:
            send(terms.at[zt, j], terms_in.at[back[zt - 1], j], col[zt - 1])

    def pass_on(j):
        arrive([passing[j]])
        send(relay_in.at[j], terms_in.at[2, j], col[0 if j in PLUS else 1])

    def blocks_of(j):
        if j in (OWN, MATE):
            return None
        return row_l.at[j], row_a.at[j]

    def run(stages, late=()):
        loads = [n for n, stage in enumerate(stages) if stage[0] is not None]

        def load(i, fn):
            b = i % 2
            for k, (src, dst) in enumerate(zip(stages[loads[i]][0], chunks[b])):
                getattr(pltpu.make_async_copy(src, dst, load_sem.at[b, k]), fn)()

        if loads:
            load(0, "start")
        gifts = list(late)
        for n, (blocks, work, after) in enumerate(stages):
            if blocks is None:
                work(None, None)
            else:
                i = loads.index(n)
                load(i, "wait")
                if i + 1 < len(loads):
                    load(i + 1, "start")
                work(*chunks[i % 2])
            for j, zt in gifts:
                give(j, zt)
            gifts = after
        return gifts

    stay = {OWN: (own_l, own_a), MATE: (mate_l, mate_a)}

    def row_stage(j, first, last):
        return (blocks_of(j), lambda l, a: row_work(j, *stay.get(j, (l, a)), first, last),
                [(j, zt) for zt in range(first, last)])

    def col_stage(rel):
        return (y_l.at[rel - 1], y_a.at[rel - 1]), lambda l, a: col_work(rel, l, a), []

    def relay(got, dsts, devs):
        out = []
        for slot, h, way in ((1, H2, 0), (0, H1, 1)):
            arrive(got[(slot, 0)])
            for dst in dsts:
                out.append(send(dst.at[slot, h], dst.at[2, h], devs[way]))
        return out

    metric_of(pno, 0)
    arrive(riders)
    pltpu.sync_copy(ints_in.at[pl.ds(0, 7)], ints_s.at[pl.ds(0, 7)])
    pltpu.sync_copy(ints, ints_s.at[7])
    pltpu.sync_copy(ints_in.at[pl.ds(7, 6)], ints_s.at[pl.ds(8, 6)])
    pltpu.sync_copy(flts, flts_s.at[0])
    pltpu.sync_copy(flts_in, flts_s.at[pl.ds(1, 3)])
    arrive(got_mate)

    def first_work(l, a):
        row_work(OWN, own_l, own_a, 0, 1)
        col_work(0, own_l, own_a)

    for cp in home:
        cp.wait()

    left = run([(None, first_work, [(OWN, 0)]), row_stage(MATE, 0, 1)])

    far_z = relay(got_z, [z_l], col)
    far_x = []
    for slot, h, way in ((1, H2, 0), (0, H1, 1)):
        arrive(got_x[(slot, 0)])
        for q in (0, 1):
            part = pl.ds((HALF if way == 0 else 0) + q * PIECE, PIECE)
            far_x.append((part, [
                send(row_l.at[slot, part], far_l0.at[part], row[way]),
                send(row_a.at[slot, part], far_a0.at[part], row[way]),
            ]))
    got_mx = []
    for slot, h in ((1, H2), (0, H1)):
        for dst in (row_l, row_a):
            got_mx.append(send(dst.at[slot, h], dst.at[4 + slot, h], mate))
    far_y = relay(got_y, [y_l, y_a], tall)
    mate_far = []

    def push(q):
        for way in (0, 1):
            part, cps = far_x[way * 2 + q]
            arrive(cps)
            for src, dst in zip(*far):
                mate_far.append(send(src.at[part], dst.at[part], mate))

    for slot in (0, 1):
        arrive(got_z[(slot, 1)])
        metric_of(z_l.at[slot], 1 + slot)
    left = run([row_stage(OWN, 1, 3), row_stage(MATE, 1, 3)], left)
    for slot, h in ((1, H1), (0, H2)):
        arrive(got_x[(slot, 1)])
        for dst in (row_l, row_a):
            got_mx.append(send(dst.at[slot, h], dst.at[4 + slot, h], mate))
    left = run([row_stage(0, 0, 3), row_stage(1, 0, 3)], left)
    arrive(got_mx)
    for slot in (0, 1):
        arrive(got_y[(slot, 1)])
    left = run([row_stage(4, 0, 3), row_stage(5, 0, 3), col_stage(1), col_stage(2)], left)
    arrive(far_z)
    metric_of(z_l.at[2], 3)
    near = (OWN, MATE, 0, 1, 4, 5)
    left = run([row_stage(j, 3, 4) for j in near], left)
    push(0)
    for j in near[:-1]:
        pass_on(j)
    for j, zt in left:
        give(j, zt)
    pass_on(near[-1])

    push(1)
    for n, j in ((0, FAR), (1, MATE_FAR)):
        if n == 1:
            arrive(mate_far)
        row_slots(j, *far[n], 3)
        row_slots(j, *far[n], 1)
        give(j, 3)
        row_slots(j, *far[n], 2)
        give(j, 1)
        row_slots(j, *far[n], 0)
        give(j, 2)
    pass_on(FAR)
    give(FAR, 0)
    give(MATE_FAR, 0)
    pass_on(MATE_FAR)
    arrive(far_y)
    run([col_stage(3)])
    for cp in local:
        cp.wait()
    for cp in live:
        cp.wait_send()
        if id(cp) not in arrived:
            cp.wait_recv()


def main(pno, amp, mix, lists):
    any_spec = pl.BlockSpec(memory_space=pl.ANY)
    shape = jax.ShapeDtypeStruct
    outs = [
        shape((8, 4, 128, 128), BF),
        shape((4, 8, 128, 128), BF),
        shape((3, 8, 4, 128, 128), BF),
        shape((8, 128), I32),
        shape((8, 128), F32),
        shape((8, 4, 128, 128), BF),
        shape((7, 32, 512, 128), BF),
        shape((7, 32, 128, 128), BF),
        shape((3, 32, 512, 128), BF),
        shape((3, 32, 512, 128), BF),
        shape((3, 32, 128, 128), BF),
        shape((13, 8, 128), I32),
        shape((3, 8, 128), F32),
    ]
    return pl.pallas_call(
        main_kernel,
        out_shape=outs,
        in_specs=[any_spec] * 12,
        out_specs=[any_spec] * len(outs),
        scratch_shapes=[pltpu.VMEM(v.shape, v.dtype) for v in lists] + [
            pltpu.VMEM((16, 128), F32),
            pltpu.VMEM((8, 128), I32),
            pltpu.VMEM((8, 128), F32),
            pltpu.VMEM((512, 512), BF),
            pltpu.VMEM((512, 512), BF),
            pltpu.VMEM((4, 32, 128, 512), BF),
            pltpu.VMEM((32, 512, 128), BF),
            pltpu.VMEM((32, 128, 128), BF),
            pltpu.VMEM((32, 512, 128), BF),
            pltpu.VMEM((32, 128, 128), BF),
            pltpu.VMEM((32, 512, 128), BF),
            pltpu.VMEM((32, 512, 128), BF),
            pltpu.VMEM((32, 128, 128), BF),
            pltpu.VMEM((32, 128, 128), BF),
            pltpu.VMEM((32, 512, 128), BF),
            pltpu.VMEM((32, 512, 128), BF),
            pltpu.VMEM((32, 128, 128), BF),
            pltpu.VMEM((32, 128, 128), BF),
            pltpu.VMEM((4, 8, 4, 128, 128), BF),
            pltpu.VMEM((4, 8, 128, 128), BF),
            pltpu.VMEM((2, 4, 512, 128), BF),
            pltpu.SMEM((14, 8, 128), I32),
            pltpu.SMEM((4, 8, 128), F32),
            pltpu.SemaphoreType.DMA((128,)),
            pltpu.SemaphoreType.DMA((128,)),
            pltpu.SemaphoreType.DMA((2, 2)),
            pltpu.SemaphoreType.DMA((2,)),
            pltpu.SemaphoreType.DMA((16,)),
            pltpu.SemaphoreType.DMA((10,)),
        ],
        compiler_params=pltpu.CompilerParams(
            collective_id=0, has_side_effects=True, vmem_limit_bytes=63 << 20
        ),
    )(pno, amp, mix, *lists)


def sum_kernel(ints, own_terms, col_terms, terms_in, out, own_v, col_v, in_v, sem):
    me = lax.axis_index("mem")
    g = lax.axis_index("grp")
    core = me % 2
    z = (me // 2) % 4
    x = me // 8
    loads = [
        pltpu.make_async_copy(own_terms, own_v, sem.at[0]),
        pltpu.make_async_copy(col_terms, col_v, sem.at[1]),
    ] + [pltpu.make_async_copy(terms_in.at[i], in_v.at[i], sem.at[2 + i]) for i in range(3)]
    for cp in loads:
        cp.start()
    out[...] = jnp.zeros_like(out)
    from_z = (0, 1, 3, 2)
    from_x = (1, 3, 2, 0, 1, 3, 2, 0)
    for zi in range(4):
        loads[zi + 1 if zi else 0].wait()
        for j in range(8):
            m = ((x + from_x[j]) % 4) * 8 + ((z + from_z[zi]) % 4) * 2 + (core + (3 <= j < 7)) % 2
            for k in range(4):
                e = m * 4 + k

                @pl.when(ints[2, e] > 0)
                def _():
                    t = ints[1, e]
                    v = own_v[j, k] if zi == 0 else in_v[zi - 1, j, k]
                    out[t] = out[t] + v.astype(F32)

        if zi == 0:
            loads[1].wait()
            for rel in range(4):
                for k in range(8):
                    e = ((g + (0, 1, 3, 2)[rel]) % 4) * 8 + k

                    @pl.when(ints[4, 64 + e] > 0)
                    def _():
                        t = ints[4, 32 + e]
                        out[t] = out[t] + col_v[rel, k].astype(F32)


def total(ints, own_terms, col_terms, terms_in):
    any_spec = pl.BlockSpec(memory_space=pl.ANY)
    return pl.pallas_call(
        sum_kernel,
        out_shape=jax.ShapeDtypeStruct((32, 128, 128), F32),
        in_specs=[pl.BlockSpec(memory_space=pltpu.SMEM)] + [any_spec] * 3,
        out_specs=pl.BlockSpec(memory_space=pltpu.VMEM),
        scratch_shapes=[
            pltpu.VMEM(own_terms.shape, BF),
            pltpu.VMEM(col_terms.shape, BF),
            pltpu.VMEM(terms_in.shape, BF),
            pltpu.SemaphoreType.DMA((5,)),
        ],
        compiler_params=pltpu.CompilerParams(vmem_limit_bytes=63 << 20),
    )(ints, own_terms, col_terms, terms_in)


def shards(
    pno, amplitudes, pno_count, pao_coupling,
    row_owner, row_pair, row_target, row_coef,
    column_owner, column_pair, column_target, column_coef,
):
    lists = [
        v.reshape(1, -1)
        for v in (
            row_owner, row_pair, row_target, row_coef, pno_count,
            column_owner, column_pair, column_target, column_coef,
        )
    ]
    own_terms, col_terms, terms_in, ints = main(pno, amplitudes, pao_coupling, lists)[:4]
    return total(ints, own_terms, col_terms, terms_in)


def solution(mesh):
    both = P(("grp", "mem"))
    in_specs = (
        P(("grp", "mem"), None, None),
        P(("grp", "mem"), None, None),
        both,
        P(),
        P(("grp", "mem"), None),
        both,
        both,
        both,
        P(("grp", "mem"), None),
        both,
        both,
        both,
    )
    out_specs = P(("grp", "mem"), None, None)
    return jax.shard_map(shards, mesh=mesh, in_specs=in_specs, out_specs=out_specs, check_vma=False)
```
